32 devices in a mesh: dp: 4 (over y, core), expert: 8 (over z, x).
Axes of the slice: x: 2, y: 2, z: 4, core: 2. Of those that a mesh axis runs over, the one named last changes fastest.
Arguments:
- tokens: bfloat16 [4096, 3584], P(('dp', 'expert')), may hold values from -6 to 6
- cotangent: bfloat16 [4096, 3584], P(('dp', 'expert')), may hold values from -0.29882812 to 0.29882812
- routes: int32 [4096, 4], P(('dp', 'expert')), may hold values from 0 to 7, all different within a row; in each aligned block of 128 rows (0 to 127, 128 to 255, ...) at most 80 rows name the same one
- route_gain: float32 [4096, 4], P(('dp', 'expert')), may hold values from 0.2 to 1
- expert_alive: int32 [8], replicated, may hold values 0 or 1
- w_gate: bfloat16 [8, 3584, 1024], P('expert'), may hold values from -0.09375 to 0.09375
- w_up: bfloat16 [8, 3584, 1024], P('expert'), may hold values from -0.09375 to 0.09375
- w_down: bfloat16 [8, 1024, 3584], P('expert'), may hold values from -0.1875 to 0.1875
Outputs:
- grad_gate: bfloat16 [8, 3584, 1024], P('expert', 'dp')
- grad_up: bfloat16 [8, 3584, 1024], P('expert', 'dp')
- grad_down: bfloat16 [8, 1024, 3584], P('expert', 'dp')
The draws below stay inside these ranges and needn't reach their ends.
Inputs may be any that keep to these rules, and one draw needn't show every extreme that they name: `routes`: in each block of 128 tokens no expert is named by more than 80 pairs.
All inputs are finite; a program needn't handle non-finite values.
Results may differ from the reference program's by a relative error of at most 0.009.
Values may be sent and summed in bfloat16 or wider, within the bound.
No kernel may reach another device: no remote copies, remote signals or barrier semaphores. Data moves between devices by JAX's collectives and lax.ppermute only.
A program may use at most 128 MiB of HBM per device.

```python
import math
import jax
import jax.numpy as jnp
import numpy as np
from jax import lax

D = 3584
FF = 1024
TOP = 4
TOK_DEV = 128
EXPERTS = 8
CAP = 80
TOKENS = 4096
N_DP = 4
N_EXPERT = 8


def with_ends(entries, rng, low, top_value):
    extent = entries.shape
    index_at = [jax.random.randint(jax.random.fold_in(rng, axis), (), 0, extent[axis]) for axis in range(len(extent))]
    entries = entries.at[tuple(index_at)].set(low)
    longest = extent.index(max(extent))
    index_at[longest] = (index_at[longest] + 1) % extent[longest]
    return entries.at[tuple(index_at)].set(top_value)


def levels(rng, shape, split, least, top_value):
    gain, own = 1.0, jax.random.fold_in(rng, 6)
    for axis_at, shards_of in split:
        heights = jnp.exp(jax.random.uniform(jax.random.fold_in(own, axis_at), (shards_of,), jnp.float32, least / len(split), top_value / len(split)))
        gain = gain * jnp.repeat(heights, shape[axis_at] // shards_of).reshape([-1 if axis == axis_at else 1 for axis in range(len(shape))])
    return gain


def routed_block(key, own, number, rows, number_of, top, reach, slope):
    order = jax.random.permutation(key, number_of)
    packed, ordinary = portions_of(number_of, rows * top, reach, slope, True), portions_of(number_of, rows * top, reach, slope, False)
    places = jnp.arange(number_of)

    def named(lengths, offset_by):
        used = int((lengths > 0).sum())
        fixed = max(1, used // 4)
        moved = fixed + (places - fixed + offset_by * (used - fixed)) % max(1, number_of - fixed)
        return jnp.zeros((number_of,), jnp.int32).at[order[jnp.where(places < fixed, places, moved)]].set(jnp.asarray(lengths, jnp.int32))

    lengths = jnp.where(number % 4 == 0, named(packed, number // 4), named(ordinary, number - number // 4 - 1))
    mixed = jax.random.permutation(jax.random.fold_in(own, 3), number_of)
    source_of, receiver = mixed[0:number_of // 2 * 2:2], mixed[1:number_of // 2 * 2:2]
    room = jnp.minimum(lengths[source_of] - 1, reach - lengths[receiver]) // 2
    room = jnp.where((source_of == order[0]) | (receiver == order[0]) | (lengths[receiver] == 0), 0, jnp.maximum(room, 0))
    moved = jax.random.randint(jax.random.fold_in(own, 4), (number_of // 2,), 0, 1 << 20) % (room + 1)
    lengths = lengths.at[source_of].add(-moved).at[receiver].add(moved)
    members = jnp.searchsorted(jnp.cumsum(lengths), jnp.arange(rows * top), side="right").astype(jnp.int32)
    table = members.reshape(top, rows).T
    table = table[jax.random.permutation(jax.random.fold_in(own, 1), rows)]
    offset_by = jax.random.randint(jax.random.fold_in(own, 2), (rows, 1), 0, top)
    return jnp.take_along_axis(table, (jnp.arange(top)[None, :] + offset_by) % top, axis=1)


def portions_of(count, total, most, skew, full):
    loads = [(1 << 20) // math.isqrt(grade ** skew) + 1 for grade in range(1, count + 1)]
    largest = most if full else min(most, max(-(-total // count), total * loads[0] // sum(loads)))
    least = 1 if total - largest >= count - 1 else 0
    given, rest = [largest] + [least] * (count - 1), total - largest - least * (count - 1)
    while rest > 0:
        candidates = [i for i in range(1, count) if given[i] < largest] or [i for i in range(1, count) if given[i] < most]
        pool, left = sum([loads[i] for i in candidates]), rest
        for i in candidates:
            more = min(most - given[i], max(1, left * loads[i] // pool), rest)
            given[i] = given[i] + more
            rest = rest - more
    return np.array(given)


def noise(stream_key, shape, spread, reach, cuts=(), held_as=jnp.bfloat16):
    values = spread * jax.random.normal(stream_key, shape, jnp.float32)
    if cuts:
        values = values * levels(stream_key, shape, cuts, -0.22, 0.18)
    return jnp.clip(values, -reach, reach).astype(held_as)


def setup_inputs(seed: int = 0) -> dict:
    seeds = jax.random.split(jax.random.key(seed), 9)
    tokens = noise(seeds[0], (TOKENS, D), 1.0, 6.0, ((0, 32),))
    cotangent = noise(seeds[1], (TOKENS, D), 0.05, 0.29882812, ((0, 32),))
    routes_keys = jax.random.split(jax.random.fold_in(seeds[2], 1), TOKENS // TOK_DEV)
    routes_turns = jax.random.permutation(jax.random.fold_in(seeds[2], 3), TOKENS // TOK_DEV)
    routes = jax.vmap(lambda own, number: routed_block(jax.random.fold_in(seeds[2], 2), own, number, TOK_DEV, EXPERTS, TOP, CAP, 2))(routes_keys, routes_turns).reshape((TOKENS, TOP))
    route_gain = jnp.clip(0.2 + 0.8 * jax.random.uniform(seeds[3], (TOKENS, TOP), jnp.float32) ** levels(seeds[3], (TOKENS, TOP), ((0, 32),), -0.2, 0.2), 0.2, 1.0)
    expert_alive = with_ends((jax.random.randint(seeds[4], (EXPERTS,), 0, 8) < 7).astype(jnp.int32), jax.random.fold_in(seeds[4], 1), 0, 1)
    w_gate = noise(seeds[5], (EXPERTS, D, FF), D ** -0.5, 0.09375, ((0, 8),))
    w_up = noise(seeds[6], (EXPERTS, D, FF), D ** -0.5, 0.09375, ((0, 8),))
    w_down = noise(seeds[7], (EXPERTS, FF, D), FF ** -0.5, 0.1875, ((0, 8),))
    return dict(tokens=tokens, cotangent=cotangent, routes=routes, route_gain=route_gain, expert_alive=expert_alive, w_gate=w_gate, w_up=w_up, w_down=w_down)


def block_slots(routes_b, gain_b, x_b, cot_b, expert_alive):
    expert_ids = jnp.arange(EXPERTS, dtype=jnp.int32)
    pair_routes = routes_b.reshape(-1)
    one_hot = (pair_routes[:, None] == expert_ids[None, :]).astype(jnp.int32) * expert_alive[None, :]
    is_live = jnp.sum(one_hot, axis=1)
    slot_index = jnp.sum((jnp.cumsum(one_hot, axis=0) - one_hot) * one_hot, axis=1)
    dest_row = jnp.where(is_live > 0, pair_routes * CAP + slot_index, EXPERTS * CAP).astype(jnp.int32)
    pair_index = jnp.arange(TOK_DEV * TOP, dtype=jnp.int32)
    source_pair = jnp.zeros((EXPERTS * CAP,), jnp.int32).at[dest_row].set(pair_index, mode="drop")
    filled = jnp.zeros((EXPERTS * CAP,), jnp.int32).at[dest_row].set(1, mode="drop")
    token_row = source_pair // TOP
    x_slots = jnp.where(filled[:, None] > 0, x_b[token_row], jnp.zeros((), x_b.dtype))
    pair_gain = jnp.where(filled > 0, gain_b.reshape(-1)[source_pair], jnp.zeros((), gain_b.dtype))
    cot_slots = (pair_gain[:, None] * cot_b[token_row].astype(gain_b.dtype)).astype(x_b.dtype)
    return x_slots, cot_slots


def contract_rows(left, right):
    return lax.dot_general(left, right, (((0,), (0,)), ((), ())), preferred_element_type=jnp.float32)


def expert_grads(x_rows, cot_rows, gate_w, up_w, down_w):
    gate_proj = jnp.dot(x_rows, gate_w, preferred_element_type=jnp.float32)
    up_proj = jnp.dot(x_rows, up_w, preferred_element_type=jnp.float32)
    sigmoid_gate = jax.nn.sigmoid(gate_proj)
    activated = gate_proj * sigmoid_gate
    hidden = (activated * up_proj).astype(x_rows.dtype)
    d_hidden = lax.dot_general(cot_rows, down_w, (((1,), (1,)), ((), ())), preferred_element_type=jnp.float32)
    d_gate = (d_hidden * up_proj * sigmoid_gate * (1.0 + gate_proj * (1.0 - sigmoid_gate))).astype(x_rows.dtype)
    d_up = (d_hidden * activated).astype(x_rows.dtype)
    return contract_rows(x_rows, d_gate), contract_rows(x_rows, d_up), contract_rows(hidden, cot_rows)


def reference(tokens, cotangent, routes, route_gain, expert_alive, w_gate, w_up, w_down):
    per_group = N_EXPERT * TOK_DEV

    def group_step(carry, group):
        begin = (group * per_group).astype(jnp.int32)
        x_g = lax.dynamic_slice_in_dim(tokens, begin, per_group, 0).reshape(N_EXPERT, TOK_DEV, D)
        c_g = lax.dynamic_slice_in_dim(cotangent, begin, per_group, 0).reshape(N_EXPERT, TOK_DEV, D)
        r_g = lax.dynamic_slice_in_dim(routes, begin, per_group, 0).reshape(N_EXPERT, TOK_DEV, TOP)
        g_g = lax.dynamic_slice_in_dim(route_gain, begin, per_group, 0).reshape(N_EXPERT, TOK_DEV, TOP)
        x_slots, cot_slots = jax.vmap(lambda a, b, c, d: block_slots(a, b, c, d, expert_alive))(r_g, g_g, x_g, c_g)
        x_rows = x_slots.reshape(N_EXPERT, EXPERTS, CAP, D).transpose(1, 0, 2, 3).reshape(EXPERTS, N_EXPERT * CAP, D)
        c_rows = cot_slots.reshape(N_EXPERT, EXPERTS, CAP, D).transpose(1, 0, 2, 3).reshape(EXPERTS, N_EXPERT * CAP, D)
        grads = lax.map(lambda a: expert_grads(a[0], a[1], a[2], a[3], a[4]), (x_rows, c_rows, w_gate, w_up, w_down))
        new_carry = tuple(acc + part.astype(jnp.bfloat16).astype(jnp.float32) for acc, part in zip(carry, grads))
        return new_carry, None

    init = (jnp.zeros((EXPERTS, D, FF), jnp.float32), jnp.zeros((EXPERTS, D, FF), jnp.float32), jnp.zeros((EXPERTS, FF, D), jnp.float32))
    sums, _ = lax.scan(group_step, init, jnp.arange(N_DP, dtype=jnp.int32))
    return (sums[0].astype(jnp.bfloat16), sums[1].astype(jnp.bfloat16), sums[2].astype(jnp.bfloat16))
```

```python
import jax
import jax.numpy as jnp
from jax import lax
from jax.sharding import PartitionSpec as P

NZ = 4
NC = 2


def contract_rows(left, right):
    return lax.dot_general(
        left, right, (((0,), (0,)), ((), ())), preferred_element_type=jnp.float32
    )


def make_per_device(n_dp, n_expert):
    nx = n_expert // NZ
    ny = n_dp // NC

    def ex(z, x):
        return z * nx + x

    def zpairs(moves):
        return [(ex(a, x), ex(b, x)) for a, b in moves for x in range(nx)]

    ends_first = zpairs([(0, 1), (1, 0), (2, 3), (3, 2)])
    middle = zpairs([(1, 2), (2, 1)])
    outward = zpairs([(1, 0), (2, 3)])

    def z_chain(block):
        a = lax.ppermute(block, "expert", ends_first)
        c_mid = lax.ppermute(block, "expert", middle)
        b_end = lax.ppermute(c_mid, "expert", outward)
        b_mid = lax.ppermute(a, "expert", middle)
        c_end = lax.ppermute(b_mid, "expert", outward)
        return [(block,), (a,), (b_end, b_mid), (c_mid, c_end)]

    def x_pairs(k):
        return [(ex(z, x), ex(z, x ^ k)) for z in range(NZ) for x in range(nx)]

    core_pairs = [(y * NC + c, y * NC + 1 - c) for y in range(ny) for c in range(NC)]

    def y_pairs(k):
        return [(y * NC + c, (y ^ k) * NC + c) for y in range(ny) for c in range(NC)]

    def join(parts):
        return parts[0] if len(parts) == 1 else parts[0] + parts[1]

    def per_device(tokens, cotangent, routes, route_gain, expert_alive, w_gate, w_up, w_down):
        tok_count, width = tokens.shape
        top_count = routes.shape[1]
        experts_all = expert_alive.shape[0]
        cap = tok_count * top_count * 5 // (4 * experts_all)
        me = lax.axis_index("expert")
        z, x = me // nx, me % nx
        d = lax.axis_index("dp")
        y, c = d // NC, d % NC

        meta = jnp.concatenate([routes.T.astype(jnp.float32), route_gain.T], axis=0)
        metas = z_chain(meta)
        toks = z_chain(tokens)
        cots = z_chain(cotangent)

        ids = jnp.stack([z * nx + (x ^ k) for k in range(nx)])
        alive = jnp.sum(
            jnp.where(ids[:, None] == jnp.arange(experts_all)[None, :], expert_alive[None, :], 0),
            axis=1,
        )
        t_iota = jnp.arange(tok_count)
        before = (t_iota[:, None] < t_iota[None, :]).astype(jnp.bfloat16)
        slots = jnp.arange(cap, dtype=jnp.float32)

        x_parts, c_parts = [], []
        for meta_s, tok_s, cot_s in zip(metas, toks, cots):
            m = join(meta_s)
            r, g = m[:top_count], m[top_count:]
            named = r[None] == ids[:, None, None].astype(jnp.float32)
            match = jnp.any(named, axis=1) & (alive[:, None] > 0)
            gain_t = jnp.sum(jnp.where(named, g[None], 0.0), axis=1)
            pos = jnp.dot(match.astype(jnp.bfloat16), before, preferred_element_type=jnp.float32)
            pick = (pos[:, None, :] == slots[None, :, None]) & match[:, None, :]
            gain_s = jnp.sum(jnp.where(pick, gain_t[:, None, :], 0.0), axis=2).reshape(nx * cap, 1)
            pick = pick.astype(jnp.bfloat16).reshape(nx * cap, tok_count)
            x_sel = jnp.dot(pick, join(tok_s), preferred_element_type=jnp.float32).astype(
                jnp.bfloat16
            )
            c_sel = (
                gain_s * jnp.dot(pick, join(cot_s), preferred_element_type=jnp.float32)
            ).astype(jnp.bfloat16)
            for sel, parts in ((x_sel, x_parts), (c_sel, c_parts)):
                sel = sel.reshape(nx, cap, width)
                parts.append(sel[0])
                for k in range(1, nx):
                    parts.append(lax.ppermute(sel[k], "expert", x_pairs(k)))
        x_rows = jnp.concatenate(x_parts, axis=0)
        cot_rows = jnp.concatenate(c_parts, axis=0)

        gate_proj = jnp.dot(x_rows, w_gate[0], preferred_element_type=jnp.float32)
        up_proj = jnp.dot(x_rows, w_up[0], preferred_element_type=jnp.float32)
        sigmoid_gate = jax.nn.sigmoid(gate_proj)
        activated = gate_proj * sigmoid_gate
        hidden = (activated * up_proj).astype(jnp.bfloat16)
        d_hidden = lax.dot_general(
            cot_rows, w_down[0], (((1,), (1,)), ((), ())), preferred_element_type=jnp.float32
        )
        d_gate = (
            d_hidden * up_proj * sigmoid_gate * (1.0 + gate_proj * (1.0 - sigmoid_gate))
        ).astype(jnp.bfloat16)
        d_up = (d_hidden * activated).astype(jnp.bfloat16)

        def reduce_over_dp(left, right):
            n = left.shape[1] // n_dp

            def part(yy, cc):
                cols = lax.dynamic_slice_in_dim(left, (yy * NC + cc) * n, n, 1)
                return contract_rows(cols, right)

            def over_cores(yy):
                send = part(yy, 1 - c).astype(jnp.bfloat16)
                recv = lax.ppermute(send, "dp", core_pairs)
                return part(yy, c) + recv.astype(jnp.float32)

            arrived = []
            for k in range(1, ny):
                total = over_cores(y ^ k).astype(jnp.bfloat16)
                arrived.append(lax.ppermute(total, "dp", y_pairs(k)))
            total = over_cores(y)
            for a in arrived:
                total = total + a.astype(jnp.float32)
            return total.astype(jnp.bfloat16)[None]

        grad_down = reduce_over_dp(hidden, cot_rows)
        grad_gate = reduce_over_dp(x_rows, d_gate)
        grad_up = reduce_over_dp(x_rows, d_up)
        return grad_gate, grad_up, grad_down

    return per_device


def solution(mesh):
    in_specs = (
        P(("dp", "expert"), None),
        P(("dp", "expert"), None),
        P(("dp", "expert"), None),
        P(("dp", "expert"), None),
        P(),
        P("expert", None, None),
        P("expert", None, None),
        P("expert", None, None),
    )
    out_specs = (P("expert", "dp", None), P("expert", "dp", None), P("expert", "dp", None))
    per_device = make_per_device(mesh.shape["dp"], mesh.shape["expert"])
    return jax.shard_map(
        per_device, mesh=mesh, in_specs=in_specs, out_specs=out_specs, check_vma=False
    )
```

```python
import jax
import jax.numpy as jnp
from jax import lax
from jax.sharding import PartitionSpec as P

NZ = 4
NC = 2


def contract_rows(left, right):
    return lax.dot_general(
        left, right, (((0,), (0,)), ((), ())), preferred_element_type=jnp.float32
    )


def after(values, *deps):
    return lax.optimization_barrier((values, deps))[0]


def make_per_device(n_dp, n_expert):
    nx = n_expert // NZ
    ny = n_dp // NC

    def ex(z, x):
        return z * nx + x

    def zpairs(moves):
        return [(ex(a, x), ex(b, x)) for a, b in moves for x in range(nx)]

    ends_first = zpairs([(0, 1), (1, 0), (2, 3), (3, 2)])
    middle = zpairs([(1, 2), (2, 1)])
    outward = zpairs([(1, 0), (2, 3)])

    def z_swap(s):
        return zpairs([(z, z ^ s) for z in range(NZ)])

    def hop1(block):
        return lax.ppermute(block, "expert", ends_first), lax.ppermute(block, "expert", middle)

    def hop2(a, c_mid):
        return lax.ppermute(c_mid, "expert", outward), lax.ppermute(a, "expert", middle)

    def hop3(b_mid):
        return lax.ppermute(b_mid, "expert", outward)

    def over_x(sel):
        out = [sel[0]]
        for k in range(1, nx):
            pairs = [(ex(z, x), ex(z, x ^ k)) for z in range(NZ) for x in range(nx)]
            out.append(lax.ppermute(sel[k], "expert", pairs))
        return out

    core_pairs = [(y * NC + c, y * NC + 1 - c) for y in range(ny) for c in range(NC)]

    def y_pairs(k):
        return [(y * NC + c, (y ^ k) * NC + c) for y in range(ny) for c in range(NC)]

    def per_device(tokens, cotangent, routes, route_gain, expert_alive, w_gate, w_up, w_down):
        tok_count, width = tokens.shape
        top_count = routes.shape[1]
        experts_all = expert_alive.shape[0]
        cap = tok_count * top_count * 5 // (4 * experts_all)
        rows = nx * cap
        me = lax.axis_index("expert")
        z, x = me // nx, me % nx
        d = lax.axis_index("dp")
        y, c = d // NC, d % NC
        half = width // ny

        meta = jnp.concatenate([routes.T.astype(jnp.float32), route_gain.T], axis=0)
        metas = [lax.ppermute(meta, "expert", z_swap(s)) for s in range(1, NZ)]
        (tokens_out,) = after((tokens,), meta)
        xa, xc = hop1(tokens_out)
        ca, cc = hop1(cotangent)

        ids = jnp.stack([z * nx + (x ^ k) for k in range(nx)])
        alive = jnp.sum(
            jnp.where(ids[:, None] == jnp.arange(experts_all)[None, :], expert_alive[None, :], 0),
            axis=1,
        )
        t_iota = jnp.arange(tok_count)
        before = (t_iota[:, None] < t_iota[None, :]).astype(jnp.bfloat16)
        places = jnp.arange(cap, dtype=jnp.float32)

        def picks(m):
            r, g = m[:top_count], m[top_count:]
            named = r[None] == ids[:, None, None].astype(jnp.float32)
            match = jnp.any(named, axis=1) & (alive[:, None] > 0)
            gain_t = jnp.sum(jnp.where(named, g[None], 0.0), axis=1)
            pos = jnp.dot(match.astype(jnp.bfloat16), before, preferred_element_type=jnp.float32)
            pick = (pos[:, None, :] == places[None, :, None]) & match[:, None, :]
            gain_s = jnp.sum(jnp.where(pick, gain_t[:, None, :], 0.0), axis=2).reshape(rows, 1)
            return pick.astype(jnp.bfloat16).reshape(rows, tok_count), gain_s

        def select_x(pick, block):
            sel = jnp.dot(pick, block, preferred_element_type=jnp.float32).astype(jnp.bfloat16)
            return sel, over_x(sel.reshape(nx, cap, width))

        def select_c(pick, gain, block):
            sel = gain * jnp.dot(pick, block, preferred_element_type=jnp.float32)
            sel = sel.astype(jnp.bfloat16)
            return sel, over_x(sel.reshape(nx, cap, width))

        def to_y(value_of):
            return [lax.ppermute(value_of(k), "dp", y_pairs(k)) for k in range(1, ny)]

        def columns(value, yy):
            return lax.dynamic_slice_in_dim(value, yy * half, half, 1)

        x_slots, c_slots, h_slots, xs_slots, d_slots = [], [], [], [], []

        def forward_x(parts):
            xr = jnp.concatenate(parts, axis=0)
            x_slots.append(xr)
            sent = to_y(lambda k: columns(xr, y ^ k))
            xs_slots.append([columns(xr, y)] + sent)
            gate = jnp.dot(xr, w_gate[0], preferred_element_type=jnp.float32)
            up = jnp.dot(xr, w_up[0], preferred_element_type=jnp.float32)
            return gate, up

        def forward_c(parts, gate, up):
            cr = jnp.concatenate(parts, axis=0)
            c_slots.append(cr)
            dh = lax.dot_general(
                cr, w_down[0], (((1,), (1,)), ((), ())), preferred_element_type=jnp.float32
            )
            sig = jax.nn.sigmoid(gate)
            act = gate * sig
            h_slots.append((act * up).astype(jnp.bfloat16))
            dg = (dh * up * sig * (1.0 + gate * (1.0 - sig))).astype(jnp.bfloat16)
            du = (dh * act).astype(jnp.bfloat16)
            both = jnp.concatenate([dg, du], axis=1)
            d_slots.append([both] + to_y(lambda k: both))
            return both

        p0, g0 = picks(meta)
        q0, x0 = select_x(p0, tokens)
        r0, c0 = select_c(p0, g0, cotangent)
        metas = after(metas, q0, r0)
        pick_of = [None] + [picks(m) for m in metas]
        x0 = after(x0, pick_of[1:])
        gu0 = forward_x(x0)
        xa, xc = after((xa, xc), gu0)
        xb_end, xb_mid = hop2(xa, xc)
        q1, x1 = select_x(pick_of[1][0], xa)
        c0 = after(c0, q1)
        d0 = forward_c(c0, *gu0)
        ca, cc = after((ca, cc), d0)
        cb_end, cb_mid = hop2(ca, cc)
        r1, c1 = select_c(*pick_of[1], ca)
        x1 = after(x1, r1)
        gu1 = forward_x(x1)
        c1 = after(c1, gu1)
        d1 = forward_c(c1, *gu1)
        xb_end, xb_mid = after((xb_end, xb_mid), d1)
        xc_end = hop3(xb_mid)
        q2, x2 = select_x(pick_of[2][0], xb_end + xb_mid)
        x2 = after(x2, q2)
        gu2 = forward_x(x2)
        cb_end, cb_mid = after((cb_end, cb_mid), gu2)
        cc_end = hop3(cb_mid)
        r2, c2 = select_c(*pick_of[2], cb_end + cb_mid)
        c2 = after(c2, r2)
        d2 = forward_c(c2, *gu2)
        xc, xc_end = after((xc, xc_end), d2)
        q3, x3 = select_x(pick_of[3][0], xc + xc_end)
        gu3 = forward_x(x3)
        cc, cc_end = after((cc, cc_end), gu3)
        r3, c3 = select_c(*pick_of[3], cc + cc_end)
        forward_c(c3, *gu3)

        cot_rows = jnp.concatenate(c_slots, axis=0)
        hidden = jnp.concatenate(h_slots, axis=0)

        def reduce_over_dp(left, right):
            n = left.shape[1] // n_dp

            def part(yy, cc):
                cols = lax.dynamic_slice_in_dim(left, (yy * NC + cc) * n, n, 1)
                return contract_rows(cols, right)

            def over_cores(yy):
                send = part(yy, 1 - c).astype(jnp.bfloat16)
                recv = lax.ppermute(send, "dp", core_pairs)
                return part(yy, c) + recv.astype(jnp.float32)

            arrived = []
            for k in range(1, ny):
                total = over_cores(y ^ k).astype(jnp.bfloat16)
                arrived.append(lax.ppermute(total, "dp", y_pairs(k)))
            total = over_cores(y)
            for a in arrived:
                total = total + a.astype(jnp.float32)
            return total.astype(jnp.bfloat16)[None]

        grad_down = reduce_over_dp(hidden, cot_rows)

        x_all = jnp.concatenate([p for s in xs_slots for p in s], axis=0)
        d_all = jnp.concatenate([p for s in d_slots for p in s], axis=0)
        n = half // NC
        ff = d_all.shape[1] // 2

        def core_sum(right):
            def part(cc):
                return contract_rows(lax.dynamic_slice_in_dim(x_all, cc * n, n, 1), right)

            recv = lax.ppermute(part(1 - c).astype(jnp.bfloat16), "dp", core_pairs)
            return (part(c) + recv.astype(jnp.float32)).astype(jnp.bfloat16)[None]

        grad_gate = core_sum(d_all[:, :ff])
        grad_up = core_sum(d_all[:, ff:])
        return grad_gate, grad_up, grad_down

    return per_device


def solution(mesh):
    in_specs = (
        P(("dp", "expert"), None),
        P(("dp", "expert"), None),
        P(("dp", "expert"), None),
        P(("dp", "expert"), None),
        P(),
        P("expert", None, None),
        P("expert", None, None),
        P("expert", None, None),
    )
    out_specs = (P("expert", "dp", None), P("expert", "dp", None), P("expert", "dp", None))
    per_device = make_per_device(mesh.shape["dp"], mesh.shape["expert"])
    return jax.shard_map(
        per_device, mesh=mesh, in_specs=in_specs, out_specs=out_specs, check_vma=False
    )
```

```python
import functools

import jax
import jax.numpy as jnp
from jax import lax
from jax.experimental import pallas as pl
from jax.experimental.pallas import tpu as pltpu
from jax.sharding import PartitionSpec as P

NZ = 4
NC = 2
F32, BF16 = jnp.float32, jnp.bfloat16
COST = pl.CostEstimate(flops=1000, bytes_accessed=1000, transcendentals=0)


LANES = 128


def params(mib):
    return pltpu.CompilerParams(vmem_limit_bytes=mib << 20)


def contract_rows(left, right):
    return lax.dot_general(left, right, (((0,), (0,)), ((), ())), preferred_element_type=F32)


def after(values, *deps):
    return lax.optimization_barrier((values, deps))[0]


def pack_kernel(routes_ref, gain_ref, tok_ref, cot_ref, out_ref):
    top = routes_ref.shape[0]
    toks, width = tok_ref.shape
    g = gain_ref[...]
    high = g.astype(BF16)
    g = g - high.astype(F32)
    mid = g.astype(BF16)
    low = (g - mid.astype(F32)).astype(BF16)
    rows = [routes_ref[...].astype(F32), high.astype(F32), mid.astype(F32), low.astype(F32)]
    total = jnp.zeros((toks, LANES), F32)
    for i, r in enumerate(rows):
        row = lax.broadcasted_iota(jnp.int32, (top, LANES), 0)
        col = lax.broadcasted_iota(jnp.int32, (top, LANES), 1)
        place = jnp.where(col == row + i * top, 1.0, 0.0).astype(BF16)
        total = total + contract_rows(r.astype(BF16), place)
    out_ref[:toks, :width] = tok_ref[...]
    out_ref[:toks, width:] = total.astype(BF16)
    out_ref[toks:, :width] = cot_ref[...]
    out_ref[toks:, width:] = jnp.zeros((toks, LANES), BF16)


def pack(tokens, cotangent, routes, gain):
    toks, width = tokens.shape
    return pl.pallas_call(
        pack_kernel,
        in_specs=[pl.BlockSpec(memory_space=pltpu.VMEM)] * 4,
        out_specs=pl.BlockSpec(memory_space=pltpu.VMEM),
        out_shape=jax.ShapeDtypeStruct((2 * toks, width + LANES), BF16),
        compiler_params=params(8),
        cost_estimate=COST,
        name="pack",
    )(routes.T, gain.T, tokens, cotangent)


def added(refs):
    value = refs[0][...]
    for r in refs[1:]:
        value = value + r[...]
    return value


def pick_kernel(ids_ref, *refs, nx, top, n_meta, n_x, n_c):
    meta_refs, refs = refs[:n_meta], refs[n_meta:]
    x_refs, c_refs, refs = refs[:n_x], refs[n_x : n_x + n_c], refs[n_x + n_c :]
    kinds = (1 if n_x else 0) + (1 if n_c else 0)
    own_refs, send_refs = refs[:kinds], refs[kinds : kinds + nx - 1]
    pick_ref, gain_ref = refs[-2:]
    cap, toks = pick_ref.shape[1:]

    @pl.when(pl.program_id(0) == 0)
    def _():
        row = lax.broadcasted_iota(jnp.int32, (4 * top, LANES), 0)
        col = lax.broadcasted_iota(jnp.int32, (4 * top, LANES), 1)
        place = jnp.where(col == row, 1.0, 0.0).astype(BF16)
        meta = lax.dot_general(
            place, added(meta_refs), (((1,), (1,)), ((), ())), preferred_element_type=F32
        )
        r = meta[0:top]
        g = (meta[top : 2 * top] + meta[2 * top : 3 * top]) + meta[3 * top :]
        row = lax.broadcasted_iota(jnp.int32, (toks, toks), 0)
        col = lax.broadcasted_iota(jnp.int32, (toks, toks), 1)
        before = jnp.where(row < col, 1.0, 0.0).astype(BF16)
        place = lax.broadcasted_iota(jnp.int32, (cap, toks), 0).astype(F32)
        for k in range(nx):
            named = r == ids_ref[0, k].astype(F32)
            alive = ids_ref[1, k].astype(F32)
            match = jnp.sum(jnp.where(named, 1.0, 0.0), axis=0, keepdims=True) * alive
            gain_t = jnp.sum(jnp.where(named, g, 0.0), axis=0, keepdims=True)
            wide = jnp.broadcast_to(match, (8, toks)).astype(BF16)
            pos = jnp.dot(wide, before, preferred_element_type=F32)[0:1]
            pick = jnp.where(place == pos, jnp.broadcast_to(match, (cap, toks)), 0.0)
            pick_ref[k] = pick.astype(BF16)
            if n_c:
                gain_ref[k] = jnp.sum(pick * gain_t, axis=1, keepdims=True)

    for i, (block_refs, weighted) in enumerate(
        ([(x_refs, False)] if n_x else []) + ([(c_refs, True)] if n_c else [])
    ):
        block = added(block_refs)
        for k in range(nx):
            sel = jnp.dot(pick_ref[k], block, preferred_element_type=F32)
            if weighted:
                sel = gain_ref[k] * sel
            if k == 0:
                own_refs[i][...] = sel.astype(BF16)
            else:
                send_refs[k - 1][i * cap : (i + 1) * cap, :] = sel.astype(BF16)


def pick_rows(ids, metas, xs, cs, nx, cap, top, width, toks):
    tile = width // 4
    kinds = (1 if xs else 0) + (1 if cs else 0)
    out = pl.pallas_call(
        functools.partial(
            pick_kernel, nx=nx, top=top, n_meta=len(metas), n_x=len(xs), n_c=len(cs)
        ),
        grid=(width // tile,),
        in_specs=[pl.BlockSpec(memory_space=pltpu.SMEM)]
        + [pl.BlockSpec((toks, LANES), lambda j: (0, width // LANES))] * len(metas)
        + [pl.BlockSpec((toks, tile), lambda j: (0, j))] * len(xs)
        + [
            pl.BlockSpec((toks, tile), lambda j, at=v.shape[0] // toks - 1: (at, j)) for v in cs
        ],
        out_specs=[pl.BlockSpec((cap, tile), lambda j: (0, j))] * kinds
        + [pl.BlockSpec((kinds * cap, tile), lambda j: (0, j))] * (nx - 1),
        out_shape=[jax.ShapeDtypeStruct((cap, width), BF16)] * kinds
        + [jax.ShapeDtypeStruct((kinds * cap, width), BF16)] * (nx - 1),
        scratch_shapes=[pltpu.VMEM((nx, cap, toks), BF16), pltpu.VMEM((nx, cap, 1), F32)],
        compiler_params=params(6),
        cost_estimate=COST,
        name="pick",
    )(ids, *metas, *xs, *cs)
    return out[:kinds], out[kinds:]


def gate_up_kernel(y_ref, *refs, parts, ny, tpy, shift):
    rows_in, (wg_ref, wu_ref) = refs[:parts], refs[parts : parts + 2]
    gate_ref, up_ref, *splits = refs[parts + 2 : parts + 4 + ny]
    joined = refs[parts + 4 + ny]
    cap, tile = rows_in[0].shape
    j = pl.program_id(0)
    for k in range(parts):
        joined[k * cap : (k + 1) * cap, :] = rows_in[k][...]
    x = joined[...]
    gate = jnp.dot(x, wg_ref[0], preferred_element_type=F32)
    up = jnp.dot(x, wu_ref[0], preferred_element_type=F32)

    @pl.when(j == 0)
    def _():
        gate_ref[...] = gate
        up_ref[...] = up

    @pl.when(j > 0)
    def _():
        gate_ref[...] += gate
        up_ref[...] += up

    for w in range(ny):
        begin = shift if w < ny - 1 else 0
        for t in range(tpy):

            @pl.when(j == w * tpy + t)
            def _(w=w, at=begin + t * tile):
                splits[w][:, at : at + tile] = x


def gate_up(y, parts, w_gate, w_up, cap, ny, shift):
    width = parts[0].shape[1]
    ff = w_gate.shape[2]
    rows = cap * len(parts)
    tile = width // 4
    tpy = 4 // ny

    def col(j, y_ref):
        return (y_ref[0] ^ ((j // tpy + 1) % ny)) * tpy + j % tpy

    sizes = [shift + width // ny] * (ny - 1) + [width // ny]
    return pl.pallas_call(
        functools.partial(gate_up_kernel, parts=len(parts), ny=ny, tpy=tpy, shift=shift),
        grid_spec=pltpu.PrefetchScalarGridSpec(
            num_scalar_prefetch=1,
            grid=(4,),
            in_specs=[pl.BlockSpec((cap, tile), lambda j, y_ref: (0, col(j, y_ref)))] * len(parts)
            + [pl.BlockSpec((1, tile, ff), lambda j, y_ref: (0, col(j, y_ref), 0))] * 2,
            out_specs=[pl.BlockSpec((rows, ff), lambda j, y_ref: (0, 0))] * 2
            + [pl.BlockSpec((rows, s), lambda j, y_ref: (0, 0)) for s in sizes],
            scratch_shapes=[pltpu.VMEM((rows, tile), BF16)],
        ),
        out_shape=[jax.ShapeDtypeStruct((rows, ff), F32)] * 2
        + [jax.ShapeDtypeStruct((rows, s), BF16) for s in sizes],
        compiler_params=params(12),
        cost_estimate=COST,
        name="gate_up",
    )(y, *parts, w_gate, w_up)


def back_kernel(*refs, parts, aliased, n_d):
    rows_in, (wd_ref, gate_ref, up_ref) = refs[:parts], refs[parts : parts + 3]
    outs = refs[parts + 3 + aliased :]
    d_refs, (hid_ref, cot_ref, acc) = outs[:n_d], outs[n_d:]
    cap = rows_in[0].shape[0]
    ff = gate_ref.shape[1]
    j = pl.program_id(0)
    for k in range(parts):
        cot_ref[k * cap : (k + 1) * cap, :] = rows_in[k][...]
    dh = lax.dot_general(
        cot_ref[...], wd_ref[0], (((1,), (1,)), ((), ())), preferred_element_type=F32
    )

    @pl.when(j == 0)
    def _():
        acc[...] = dh

    @pl.when(j > 0)
    def _():
        acc[...] += dh

    @pl.when(j == pl.num_programs(0) - 1)
    def _():
        gate, up, total = gate_ref[...], up_ref[...], acc[...]
        sig = jax.nn.sigmoid(gate)
        act = gate * sig
        hid_ref[...] = (act * up).astype(BF16)
        d_gate = (total * up * sig * (1.0 + gate * (1.0 - sig))).astype(BF16)
        d_up = (total * act).astype(BF16)
        for d_ref in d_refs:
            d_ref[:, :ff] = d_gate
            d_ref[:, ff:] = d_up


def back(parts, at, w_down, gate, up, behind, joined, slot, cap):
    width = parts[0].shape[1]
    rows, ff = gate.shape
    tile = width // 4
    n = len(parts)
    n_d = max(len(behind), 1)
    d_shapes = [b.shape for b in behind] or [(rows, 2 * ff)]
    first = 0 if behind else 1
    aliased = [*behind, *joined]
    return pl.pallas_call(
        functools.partial(back_kernel, parts=n, aliased=len(aliased), n_d=n_d),
        grid=(4,),
        in_specs=[pl.BlockSpec((cap, tile), lambda j: (0, j))]
        + [pl.BlockSpec((cap, tile), lambda j: (at, j))] * (n - 1)
        + [pl.BlockSpec((1, ff, tile), lambda j: (0, 0, j))]
        + [pl.BlockSpec((rows, ff), lambda j: (0, 0))] * 2
        + [pl.BlockSpec(memory_space=pl.ANY)] * len(aliased),
        out_specs=[pl.BlockSpec((rows, 2 * ff), lambda j: (0, 0))] * n_d
        + [
            pl.BlockSpec((rows, ff), lambda j: (slot, 0)),
            pl.BlockSpec((rows, tile), lambda j: (slot, j)),
        ],
        out_shape=[jax.ShapeDtypeStruct(s, BF16) for s in d_shapes]
        + [
            jax.ShapeDtypeStruct((NZ * rows, ff), BF16),
            jax.ShapeDtypeStruct((NZ * rows, width), BF16),
        ],
        scratch_shapes=[pltpu.VMEM((rows, ff), F32)],
        input_output_aliases={n + 3 + i: first + i for i in range(len(aliased))},
        compiler_params=params(11),
        cost_estimate=COST,
        name="back",
    )(*parts, w_down, gate, up, *aliased)


def down_kernel(s_ref, hid_ref, cot_ref, *refs, chunks, outs):
    ins, out_refs, acc = refs[: sum(chunks)], refs[-1 - outs : -1], refs[-1]
    j, steps = pl.program_id(0), pl.num_programs(0)
    acc[...] = contract_rows(hid_ref[...], cot_ref[...])
    i = 0
    for count in chunks:
        for w in range(count):

            @pl.when(j * count // steps == w)
            def _(ref=ins[i]):
                acc[...] += ref[...].astype(F32)

            i += 1
    for w in range(outs):

        @pl.when(j * outs // steps == w)
        def _(w=w):
            out_refs[w][...] = acc[...].astype(BF16)


def down_part(index, hidden, cot, n, arrived=(), outs=1):
    k, width = cot.shape
    steps = 4
    tile = width // steps

    def chunk(w, count):
        per = steps // count
        return pl.BlockSpec(
            (n, tile), lambda j, s_ref: (0, jnp.minimum(jnp.maximum(j - w * per, 0), per - 1))
        )

    return pl.pallas_call(
        functools.partial(down_kernel, chunks=tuple(len(a) for a in arrived), outs=outs),
        grid_spec=pltpu.PrefetchScalarGridSpec(
            num_scalar_prefetch=1,
            grid=(steps,),
            in_specs=[
                pl.BlockSpec((k, n), lambda j, s_ref: (0, s_ref[0])),
                pl.BlockSpec((k, tile), lambda j, s_ref: (0, j)),
            ]
            + [chunk(w, len(a)) for a in arrived for w in range(len(a))],
            out_specs=[chunk(w, outs) for w in range(outs)],
            scratch_shapes=[pltpu.VMEM((n, tile), F32)],
        ),
        out_shape=[jax.ShapeDtypeStruct((n, width // outs), BF16)] * outs,
        compiler_params=params(9),
        cost_estimate=COST,
        name="down_part",
    )(index, hidden, cot, *[piece for a in arrived for piece in a])


def both_kernel(c_ref, *refs, pieces, add):
    xs, ds = refs[:pieces], refs[pieces : 2 * pieces]
    rest = refs[2 * pieces :]
    got, outs, (left, right, acc) = rest[:add], rest[add:-3], rest[-3:]
    rows = xs[0].shape[0]
    j = pl.program_id(0)

    @pl.when(j == 0)
    def _():
        for i in range(pieces):
            left[i * rows : (i + 1) * rows, :] = xs[i][...]

    for i in range(pieces):
        right[i * rows : (i + 1) * rows, :] = ds[i][...]
    acc[...] = contract_rows(left[...], right[...])
    for w, out in enumerate(outs):

        @pl.when(j * len(outs) // pl.num_programs(0) == w)
        def _(w=w, out=out):
            total = acc[...]
            if add:
                total = total + got[w][...].astype(F32)
            out[...] = total.astype(BF16)


def both_part(index, xs, ds, n, ff2, half, arrived=()):
    rows = ds[0].shape[0]
    steps, tile = 4, ff2 // 4
    m = len(xs)
    add = len(arrived)
    outs = 2
    per = steps // outs
    pair = [
        pl.BlockSpec(
            (n, tile),
            lambda j, c_ref, w=w: (0, jnp.minimum(jnp.maximum(j - w * per, 0), per - 1)),
        )
        for w in range(outs)
    ]

    def x_spec(value):
        begin = value.shape[1] - half
        if begin == 0:
            return pl.BlockSpec((rows, n), lambda j, c_ref: (0, c_ref[0]))
        return pl.BlockSpec(
            (pl.Element(rows), pl.Element(n)),
            lambda j, c_ref: (0, pl.multiple_of(begin + c_ref[0] * n, LANES)),
        )

    return pl.pallas_call(
        functools.partial(both_kernel, pieces=m, add=add),
        grid_spec=pltpu.PrefetchScalarGridSpec(
            num_scalar_prefetch=1,
            grid=(steps,),
            in_specs=[x_spec(v) for v in xs]
            + [pl.BlockSpec((rows, tile), lambda j, c_ref: (0, j))] * m
            + pair[:add],
            out_specs=pair,
            scratch_shapes=[
                pltpu.VMEM((m * rows, n), BF16),
                pltpu.VMEM((m * rows, tile), BF16),
                pltpu.VMEM((n, tile), F32),
            ],
        ),
        out_shape=[jax.ShapeDtypeStruct((n, ff2 // outs), BF16)] * outs,
        compiler_params=params(22),
        cost_estimate=COST,
        name="both_part",
    )(index, *xs, *ds, *arrived)


def make_per_device(n_dp, n_expert):
    nx = n_expert // NZ
    ny = n_dp // NC

    def ex(z, x):
        return z * nx + x

    def zpairs(moves):
        return [(ex(a, x), ex(b, x)) for a, b in moves for x in range(nx)]

    ends_first = zpairs([(0, 1), (1, 0), (2, 3), (3, 2)])
    middle = zpairs([(1, 2), (2, 1)])
    outward = zpairs([(1, 0), (2, 3)])

    def hop1(block):
        return lax.ppermute(block, "expert", ends_first), lax.ppermute(block, "expert", middle)

    def hop2(a, c_mid):
        return lax.ppermute(c_mid, "expert", outward), lax.ppermute(a, "expert", middle)

    def hop3(b_mid):
        return lax.ppermute(b_mid, "expert", outward)

    def over_x(sends):
        out = []
        for k in range(1, nx):
            pairs = [(ex(z, x), ex(z, x ^ k)) for z in range(NZ) for x in range(nx)]
            out.append(lax.ppermute(sends[k - 1], "expert", pairs))
        return out

    core_pairs = [(y * NC + c, y * NC + 1 - c) for y in range(ny) for c in range(NC)]

    def over_core(value):
        return lax.ppermute(value, "dp", core_pairs)

    def over_y(value, k):
        return lax.ppermute(
            value, "dp", [(y * NC + c, (y ^ k) * NC + c) for y in range(ny) for c in range(NC)]
        )

    def per_device(tokens, cotangent, routes, route_gain, expert_alive, w_gate, w_up, w_down):
        tok_count, width = tokens.shape
        top = routes.shape[1]
        experts_all = expert_alive.shape[0]
        cap = tok_count * top * 5 // (4 * experts_all)
        ff = w_gate.shape[2]
        half = width // ny
        me = lax.axis_index("expert")
        z, x = me // nx, me % nx
        d = lax.axis_index("dp")
        y_arr = (d // NC).astype(jnp.int32)[None]
        c_arr = (d % NC).astype(jnp.int32)[None]

        own = pack(tokens, cotangent, routes, route_gain)
        a, c_mid = hop1(own)

        own_ids = z * nx + (x ^ jnp.arange(nx, dtype=jnp.int32))
        alive = jnp.sum(
            jnp.where(
                own_ids[:, None] == jnp.arange(experts_all)[None, :], expert_alive[None, :], 0
            ),
            axis=1,
        )
        ids = jnp.stack([own_ids, alive.astype(jnp.int32)])

        def pick(metas, xs=(), cs=()):
            own, sends = pick_rows(ids, metas, xs, cs, nx, cap, top, width, tok_count)
            return own, over_x(sends)

        x_own, x_got, d_own, d_got, joined = [], [], [], [], []

        def forward(parts, shift):
            gate, up, *splits = gate_up(y_arr, parts, w_gate, w_up, cap, ny, shift)
            x_own.append(splits[-1])
            return gate, up, splits[:-1]

        def backward(parts, at, gate, up, behind, slot):
            out = back(parts, at, w_down, gate, up, behind, joined, slot, cap)
            joined[:] = out[-2:]
            return out[:-2]

        def exchange(filled):
            d_own.append(filled[0])
            got = [over_y(f, k) for k, f in zip(range(1, ny), filled)]
            x_got.append(got)
            d_got.append(got)
            return got

        (x0,), s0 = pick([own], [own])
        (c0,), t0 = pick([own], (), [after(own, x0)])
        s0 = after(s0, c0)
        g0, u0, b0 = forward([x0, *s0], 2 * ff)
        f0 = backward([c0, *t0], 0, g0, u0, b0, 0)
        y0 = exchange(f0)
        a, c_mid = after((a, c_mid), f0)
        b_end, b_mid = hop2(a, c_mid)
        (x1, c1), s1 = pick([a], [a], [a])
        s1 = after(s1, y0)
        g1, u1, b1 = forward([x1, *s1], 2 * ff)
        f1 = backward([c1, *s1], 1, g1, u1, b1, 1)
        y1 = exchange(f1)
        xc_end = hop3(b_mid[:tok_count])
        cc_end = hop3(b_mid[tok_count:, :width])
        b_end, b_mid = after((b_end, b_mid), f1)
        (x2,), s2 = pick([b_end, b_mid], [b_end, b_mid])
        (c2,), t2 = pick([b_end, b_mid], (), after([b_end, b_mid], x2))
        s2 = after(s2, c2)
        g2, u2, b2 = forward([x2, *s2], 2 * ff)
        c_mid, xc_end = after((c_mid, xc_end), g2, y1)
        (x3,), s3 = pick([c_mid, xc_end], [c_mid, xc_end])
        t2 = after(t2, x3)
        f2 = backward([c2, *t2], 0, g2, u2, b2, 2)
        y2 = exchange(f2)
        s3 = after(s3, f2)
        g3, u3, b3 = forward([x3, *s3], 0)
        x_got.append([over_y(b, k) for k, b in zip(range(1, ny), b3)])
        cc_end = after(cc_end, g3)
        (c3,), t3 = pick([c_mid, xc_end], (), [c_mid, cc_end])
        t3 = after(t3, c3, y2, x_got[-1])
        (f3,) = backward([c3, *t3], 0, g3, u3, [], 3)
        d_own.append(f3)
        d_got.append([over_y(f3, k) for k in range(1, ny)])

        hidden, cot_rows = joined
        n = ff // n_dp

        def to_core(yy):
            return over_core(down_part(yy * NC + (1 - c_arr), hidden, cot_rows, n)[0])

        landed, totals = [], []
        for k in range(1, ny):
            recv = to_core(y_arr ^ k)
            first, second = down_part(
                (y_arr ^ k) * NC + c_arr, hidden, cot_rows, n, [[recv]], outs=2
            )
            first = over_y(first, k)
            landed.append([first, over_y(after(second, first), k)])
            totals.append(second)

        m = half // NC
        xs, ds = [], []
        for s in range(NZ):
            xs += [x_own[s], *x_got[s]]
            ds += [d_own[s], *d_got[s]]
        if m % LANES == 0:
            ds[0] = after(ds[0], totals)
            recv = [over_core(v) for v in both_part(1 - c_arr, xs, ds, m, 2 * ff, half)]
            own_recv = to_core(y_arr)
            grad_gate, grad_up = both_part(c_arr, xs, ds, m, 2 * ff, half, recv)
        else:
            x_all = jnp.concatenate([v[:, v.shape[1] - half :] for v in xs], axis=0)
            d_all = jnp.concatenate([v[:, : 2 * ff] for v in ds], axis=0)

            def part(c):
                return contract_rows(lax.dynamic_slice_in_dim(x_all, c * m, m, 1), d_all)

            recv = over_core(part(1 - c_arr[0]).astype(BF16))
            own_recv = to_core(y_arr)
            total = (part(c_arr[0]) + recv.astype(F32)).astype(BF16)
            grad_gate, grad_up = total[:, :ff], total[:, ff:]

        (grad_down,) = down_part(
            y_arr * NC + c_arr, hidden, cot_rows, n, [[own_recv], *landed]
        )
        return grad_gate[None], grad_up[None], grad_down[None]

    return per_device


def solution(mesh):
    in_specs = (
        P(("dp", "expert"), None),
        P(("dp", "expert"), None),
        P(("dp", "expert"), None),
        P(("dp", "expert"), None),
        P(),
        P("expert", None, None),
        P("expert", None, None),
        P("expert", None, None),
    )
    out_specs = (P("expert", "dp", None), P("expert", "dp", None), P("expert", "dp", None))
    per_device = make_per_device(mesh.shape["dp"], mesh.shape["expert"])
    return jax.shard_map(
        per_device, mesh=mesh, in_specs=in_specs, out_specs=out_specs, check_vma=False
    )
```

```python
import functools

import jax
import jax.numpy as jnp
from jax import lax
from jax.experimental import pallas as pl
from jax.experimental.pallas import tpu as pltpu
from jax.sharding import PartitionSpec as P

NZ = 4
NC = 2
F32, BF16 = jnp.float32, jnp.bfloat16
COST = pl.CostEstimate(flops=3000000000, bytes_accessed=1000, transcendentals=0)


LANES = 128


def params(mib):
    return pltpu.CompilerParams(vmem_limit_bytes=mib << 20)


def contract_rows(left, right):
    return lax.dot_general(left, right, (((0,), (0,)), ((), ())), preferred_element_type=F32)


def after(values, *deps):
    return lax.optimization_barrier((values, deps))[0]


def pack_kernel(routes_ref, gain_ref, tok_ref, cot_ref, out_ref):
    top = routes_ref.shape[0]
    toks, width = tok_ref.shape
    g = gain_ref[...]
    high = g.astype(BF16)
    g = g - high.astype(F32)
    mid = g.astype(BF16)
    low = (g - mid.astype(F32)).astype(BF16)
    rows = [routes_ref[...].astype(F32), high.astype(F32), mid.astype(F32), low.astype(F32)]
    total = jnp.zeros((toks, LANES), F32)
    for i, r in enumerate(rows):
        row = lax.broadcasted_iota(jnp.int32, (top, LANES), 0)
        col = lax.broadcasted_iota(jnp.int32, (top, LANES), 1)
        place = jnp.where(col == row + i * top, 1.0, 0.0).astype(BF16)
        total = total + contract_rows(r.astype(BF16), place)
    out_ref[:toks, :width] = tok_ref[...]
    out_ref[:toks, width:] = total.astype(BF16)
    out_ref[toks:, :width] = cot_ref[...]
    out_ref[toks:, width:] = jnp.zeros((toks, LANES), BF16)


def pack(tokens, cotangent, routes, gain):
    toks, width = tokens.shape
    return pl.pallas_call(
        pack_kernel,
        in_specs=[pl.BlockSpec(memory_space=pltpu.VMEM)] * 4,
        out_specs=pl.BlockSpec(memory_space=pltpu.VMEM),
        out_shape=jax.ShapeDtypeStruct((2 * toks, width + LANES), BF16),
        compiler_params=params(8),
        cost_estimate=COST,
        name="pack",
    )(routes.T, gain.T, tokens, cotangent)


def added(refs):
    value = refs[0][...]
    for r in refs[1:]:
        value = value + r[...]
    return value


def pick_kernel(ids_ref, *refs, nx, top, n_meta, n_x, n_c):
    meta_refs, refs = refs[:n_meta], refs[n_meta:]
    x_refs, c_refs, refs = refs[:n_x], refs[n_x : n_x + n_c], refs[n_x + n_c :]
    kinds = (1 if n_x else 0) + (1 if n_c else 0)
    own_refs, send_refs = refs[:kinds], refs[kinds : kinds + nx - 1]
    pick_ref, gain_ref = refs[-2:]
    cap, toks = pick_ref.shape[1:]

    @pl.when(pl.program_id(0) == 0)
    def _():
        row = lax.broadcasted_iota(jnp.int32, (4 * top, LANES), 0)
        col = lax.broadcasted_iota(jnp.int32, (4 * top, LANES), 1)
        place = jnp.where(col == row, 1.0, 0.0).astype(BF16)
        meta = lax.dot_general(
            place, added(meta_refs), (((1,), (1,)), ((), ())), preferred_element_type=F32
        )
        r = meta[0:top]
        g = (meta[top : 2 * top] + meta[2 * top : 3 * top]) + meta[3 * top :]
        row = lax.broadcasted_iota(jnp.int32, (toks, toks), 0)
        col = lax.broadcasted_iota(jnp.int32, (toks, toks), 1)
        before = jnp.where(row < col, 1.0, 0.0).astype(BF16)
        place = lax.broadcasted_iota(jnp.int32, (cap, toks), 0).astype(F32)
        for k in range(nx):
            named = r == ids_ref[0, k].astype(F32)
            alive = ids_ref[1, k].astype(F32)
            match = jnp.sum(jnp.where(named, 1.0, 0.0), axis=0, keepdims=True) * alive
            gain_t = jnp.sum(jnp.where(named, g, 0.0), axis=0, keepdims=True)
            wide = jnp.broadcast_to(match, (8, toks)).astype(BF16)
            pos = jnp.dot(wide, before, preferred_element_type=F32)[0:1]
            pick = jnp.where(place == pos, jnp.broadcast_to(match, (cap, toks)), 0.0)
            pick_ref[k] = pick.astype(BF16)
            if n_c:
                gain_ref[k] = jnp.sum(pick * gain_t, axis=1, keepdims=True)

    for i, (block_refs, weighted) in enumerate(
        ([(x_refs, False)] if n_x else []) + ([(c_refs, True)] if n_c else [])
    ):
        block = added(block_refs)
        for k in range(nx):
            sel = jnp.dot(pick_ref[k], block, preferred_element_type=F32)
            if weighted:
                sel = gain_ref[k] * sel
            if k == 0:
                own_refs[i][...] = sel.astype(BF16)
            else:
                send_refs[k - 1][i * cap : (i + 1) * cap, :] = sel.astype(BF16)


def pick_rows(ids, metas, xs, cs, nx, cap, top, width, toks):
    tile = width // 4
    kinds = (1 if xs else 0) + (1 if cs else 0)
    own, *sends = pl.pallas_call(
        functools.partial(
            pick_kernel, nx=nx, top=top, n_meta=len(metas), n_x=len(xs), n_c=len(cs)
        ),
        grid=(width // tile,),
        in_specs=[pl.BlockSpec(memory_space=pltpu.SMEM)]
        + [pl.BlockSpec((toks, LANES), lambda j: (0, width // LANES))] * len(metas)
        + [pl.BlockSpec((toks, tile), lambda j: (0, j))] * len(xs)
        + [
            pl.BlockSpec((toks, tile), lambda j, at=v.shape[0] // toks - 1: (at, j)) for v in cs
        ],
        out_specs=[pl.BlockSpec((cap, tile), lambda j: (0, j))] * kinds
        + [pl.BlockSpec((kinds * cap, tile), lambda j: (0, j))] * (nx - 1),
        out_shape=[jax.ShapeDtypeStruct((cap, width), BF16)] * kinds
        + [jax.ShapeDtypeStruct((kinds * cap, width), BF16)] * (nx - 1),
        scratch_shapes=[pltpu.VMEM((nx, cap, toks), BF16), pltpu.VMEM((nx, cap, 1), F32)],
        compiler_params=params(6),
        cost_estimate=COST,
        name="pick",
    )(ids, *metas, *xs, *cs)
    return own, sends


def whole(count):
    return [pl.BlockSpec(memory_space=pltpu.VMEM)] * count


def gate_up_kernel(y_ref, *refs, parts, ny):
    rows_in, (wg_ref, wu_ref) = refs[:parts], refs[parts : parts + 2]
    gate_ref, up_ref, *splits = refs[parts + 2 : parts + 4 + ny]
    joined = refs[parts + 4 + ny]
    cap = rows_in[0].shape[0]
    for k in range(parts):
        joined[k * cap : (k + 1) * cap, :] = rows_in[k][...]
    half = joined.shape[1] // ny
    for k in range(ny):
        begin = pl.multiple_of((y_ref[0] ^ k) * half, LANES)
        splits[k][...] = joined[:, pl.ds(begin, half)]
    x = joined[...]
    gate_ref[...] = jnp.dot(x, wg_ref[0], preferred_element_type=F32)
    up_ref[...] = jnp.dot(x, wu_ref[0], preferred_element_type=F32)


def gate_up(y, parts, w_gate, w_up, ny):
    cap, width = parts[0].shape
    ff = w_gate.shape[2]
    rows = cap * len(parts)
    return pl.pallas_call(
        functools.partial(gate_up_kernel, parts=len(parts), ny=ny),
        in_specs=[pl.BlockSpec(memory_space=pltpu.SMEM)] + whole(len(parts) + 2),
        out_specs=whole(2 + ny),
        out_shape=[jax.ShapeDtypeStruct((rows, ff), F32)] * 2
        + [jax.ShapeDtypeStruct((rows, width // ny), BF16)] * ny,
        scratch_shapes=[pltpu.VMEM((rows, width), BF16)],
        compiler_params=params(10),
        cost_estimate=COST,
        name="gate_up",
    )(y, *parts, w_gate, w_up)


def back_kernel(*refs, parts):
    rows_in, (wd_ref, gate_ref, up_ref) = refs[:parts], refs[parts : parts + 3]
    d_ref, hid_ref, cot_ref = refs[parts + 3 :]
    cap = rows_in[0].shape[0]
    ff = gate_ref.shape[1]
    for k in range(parts):
        cot_ref[k * cap : (k + 1) * cap, :] = rows_in[k][...]
    total = lax.dot_general(
        cot_ref[...], wd_ref[0], (((1,), (1,)), ((), ())), preferred_element_type=F32
    )
    gate, up = gate_ref[...], up_ref[...]
    sig = jax.nn.sigmoid(gate)
    act = gate * sig
    hid_ref[...] = (act * up).astype(BF16)
    d_ref[:, :ff] = (total * up * sig * (1.0 + gate * (1.0 - sig))).astype(BF16)
    d_ref[:, ff:] = (total * act).astype(BF16)


def back(parts, w_down, gate, up):
    width = parts[0].shape[1]
    rows, ff = gate.shape
    n = len(parts)
    return pl.pallas_call(
        functools.partial(back_kernel, parts=n),
        in_specs=whole(n + 3),
        out_specs=whole(3),
        out_shape=[
            jax.ShapeDtypeStruct((rows, 2 * ff), BF16),
            jax.ShapeDtypeStruct((rows, ff), BF16),
            jax.ShapeDtypeStruct((rows, width), BF16),
        ],
        compiler_params=params(10),
        cost_estimate=COST,
        name="back",
    )(*parts, w_down, gate, up)


def down_kernel(s_ref, *refs, pieces, ins, outs):
    hids, cots, refs = refs[:pieces], refs[pieces : 2 * pieces], refs[2 * pieces :]
    in_refs, out_refs, (left, right, acc) = refs[: len(ins)], refs[len(ins) : -3], refs[-3:]
    j = pl.program_id(0)
    rows = hids[0].shape[0]
    for k in range(pieces):
        left[k * rows : (k + 1) * rows, :] = hids[k][...]
        right[k * rows : (k + 1) * rows, :] = cots[k][...]
    acc[...] = contract_rows(left[...], right[...])
    for (begin, size), ref in zip(ins, in_refs):

        @pl.when((j >= begin) & (j < begin + size))
        def _(ref=ref):
            acc[...] += ref[...].astype(F32)

    for (begin, size), ref in zip(outs, out_refs):

        @pl.when((j >= begin) & (j < begin + size))
        def _(ref=ref):
            ref[...] = acc[...].astype(ref.dtype)


def down_part(index, hidden, cot, n, arrived=(), outs=(4,), dtype=BF16):
    rows, width = cot[0].shape
    m = len(cot)
    steps = 4
    tile = width // steps

    def ranges(sizes):
        return [(sum(sizes[:i]), size) for i, size in enumerate(sizes)]

    def chunk(begin, size):
        return pl.BlockSpec(
            (n, tile), lambda j, s_ref: (0, jnp.minimum(jnp.maximum(j - begin, 0), size - 1))
        )

    ins = [r for a in arrived for r in ranges([v.shape[1] // tile for v in a])]
    outs = ranges(outs)
    return pl.pallas_call(
        functools.partial(down_kernel, pieces=m, ins=ins, outs=outs),
        grid_spec=pltpu.PrefetchScalarGridSpec(
            num_scalar_prefetch=1,
            grid=(steps,),
            in_specs=[pl.BlockSpec((rows, n), lambda j, s_ref: (0, s_ref[0]))] * m
            + [pl.BlockSpec((rows, tile), lambda j, s_ref: (0, j))] * m
            + [chunk(*r) for r in ins],
            out_specs=[chunk(*r) for r in outs],
            scratch_shapes=[
                pltpu.VMEM((m * rows, n), BF16),
                pltpu.VMEM((m * rows, tile), BF16),
                pltpu.VMEM((n, tile), F32),
            ],
        ),
        out_shape=[jax.ShapeDtypeStruct((n, tile * size), dtype) for _, size in outs],
        compiler_params=params(9),
        cost_estimate=COST,
        name="down_part",
    )(index, *hidden, *cot, *[piece for a in arrived for piece in a])


def both_kernel(c_ref, *refs, pieces, add):
    xs, ds = refs[:pieces], refs[pieces : 2 * pieces]
    rest = refs[2 * pieces :]
    got, outs, (left, right, acc) = rest[:add], rest[add:-3], rest[-3:]
    rows = xs[0].shape[0]
    j = pl.program_id(0)

    @pl.when(j == 0)
    def _():
        for i in range(pieces):
            left[i * rows : (i + 1) * rows, :] = xs[i][...]

    for i in range(pieces):
        right[i * rows : (i + 1) * rows, :] = ds[i][...]
    acc[...] = contract_rows(left[...], right[...])
    for w, ref in enumerate(got):

        @pl.when(j == w)
        def _(ref=ref):
            acc[...] += ref[...].astype(F32)

    for w, out in enumerate(outs):

        @pl.when(j * len(outs) // pl.num_programs(0) == w)
        def _(w=w, out=out):
            total = acc[...]
            out[...] = total.astype(BF16)


def both_part(index, xs, ds, n, arrived=()):
    rows, ff2 = ds[0].shape
    steps, tile = 4, ff2 // 4
    m = len(xs)
    add = len(arrived)
    outs = 2 if add else steps
    per = steps // outs

    return pl.pallas_call(
        functools.partial(both_kernel, pieces=m, add=add),
        grid_spec=pltpu.PrefetchScalarGridSpec(
            num_scalar_prefetch=1,
            grid=(steps,),
            in_specs=[pl.BlockSpec((rows, n), lambda j, c_ref: (0, c_ref[0]))] * m
            + [pl.BlockSpec((rows, tile), lambda j, c_ref: (0, j))] * m
            + [pl.BlockSpec((n, tile), lambda j, c_ref: (0, 0))] * add,
            out_specs=[
                pl.BlockSpec(
                    (n, tile),
                    lambda j, c_ref, w=w: (0, jnp.minimum(jnp.maximum(j - w * per, 0), per - 1)),
                )
                for w in range(outs)
            ],
            scratch_shapes=[
                pltpu.VMEM((m * rows, n), BF16),
                pltpu.VMEM((m * rows, tile), BF16),
                pltpu.VMEM((n, tile), F32),
            ],
        ),
        out_shape=[jax.ShapeDtypeStruct((n, ff2 // outs), BF16)] * outs,
        compiler_params=params(22),
        cost_estimate=COST,
        name="both_part",
    )(index, *xs, *ds, *arrived)


def make_per_device(n_dp, n_expert):
    nx = n_expert // NZ
    ny = n_dp // NC

    def ex(z, x):
        return z * nx + x

    def zpairs(moves):
        return [(ex(a, x), ex(b, x)) for a, b in moves for x in range(nx)]

    ends_first = zpairs([(0, 1), (1, 0), (2, 3), (3, 2)])
    middle = zpairs([(1, 2), (2, 1)])
    outward = zpairs([(1, 0), (2, 3)])

    def hop1(block):
        return lax.ppermute(block, "expert", ends_first), lax.ppermute(block, "expert", middle)

    def hop2(a, c_mid):
        return lax.ppermute(c_mid, "expert", outward), lax.ppermute(a, "expert", middle)

    def hop3(b_mid):
        return lax.ppermute(b_mid, "expert", outward)

    def over_x(sends):
        out = []
        for k in range(1, nx):
            pairs = [(ex(z, x), ex(z, x ^ k)) for z in range(NZ) for x in range(nx)]
            out.append(lax.ppermute(sends[k - 1], "expert", pairs))
        return out

    core_pairs = [(y * NC + c, y * NC + 1 - c) for y in range(ny) for c in range(NC)]

    def over_core(value):
        return lax.ppermute(value, "dp", core_pairs)

    def over_y(value, k):
        return lax.ppermute(
            value, "dp", [(y * NC + c, (y ^ k) * NC + c) for y in range(ny) for c in range(NC)]
        )

    def per_device(tokens, cotangent, routes, route_gain, expert_alive, w_gate, w_up, w_down):
        tok_count, width = tokens.shape
        top = routes.shape[1]
        experts_all = expert_alive.shape[0]
        cap = tok_count * top * 5 // (4 * experts_all)
        ff = w_gate.shape[2]
        half = width // ny
        me = lax.axis_index("expert")
        z, x = me // nx, me % nx
        d = lax.axis_index("dp")
        y_arr = (d // NC).astype(jnp.int32)[None]
        c_arr = (d % NC).astype(jnp.int32)[None]

        own = pack(tokens, cotangent, routes, route_gain)
        a, c_mid = hop1(own)

        own_ids = z * nx + (x ^ jnp.arange(nx, dtype=jnp.int32))
        alive = jnp.sum(
            jnp.where(
                own_ids[:, None] == jnp.arange(experts_all)[None, :], expert_alive[None, :], 0
            ),
            axis=1,
        )
        ids = jnp.stack([own_ids, alive.astype(jnp.int32)])

        def pick(metas, xs=(), cs=()):
            own, sends = pick_rows(ids, metas, xs, cs, nx, cap, top, width, tok_count)
            return own, over_x(sends)

        xs, ds, hidden, cot_rows = [], [], [], []

        def spread(pieces, values):
            got = [over_y(values[k], k) for k in range(1, ny)]
            pieces += [values[0], *got]
            return got

        def forward(parts):
            gate, up, *splits = gate_up(y_arr, parts, w_gate, w_up, ny)
            return gate, up, spread(xs, splits)

        def backward(parts, gate, up):
            both, hid, cot = back(parts, w_down, gate, up)
            hidden.append(hid)
            cot_rows.append(cot)
            return both, spread(ds, [both] * ny)

        x0, s0 = pick([own], [own])
        c0, t0 = pick([own], (), [after(own, x0)])
        g0, u0, xs0 = forward([x0, *s0])
        f0, d0 = backward([c0, *t0], g0, u0)
        a, c_mid = after((a, c_mid), f0)
        b_end, b_mid = hop2(a, c_mid)
        x1, s1 = pick([a], [a])
        c1, t1 = pick([a], (), [after(a, x1)])
        s1 = after(s1, c1, xs0)
        g1, u1, xs1 = forward([x1, *s1])
        t1 = after(t1, d0)
        f1, d1 = backward([c1, *t1], g1, u1)
        xc_end = hop3(b_mid[:tok_count])
        cc_end = hop3(b_mid[tok_count:, :width])
        b_end, b_mid = after((b_end, b_mid), f1)
        x2, s2 = pick([b_end, b_mid], [b_end, b_mid])
        c2, t2 = pick([b_end, b_mid], (), after([b_end, b_mid], x2))
        s2 = after(s2, c2, xs1)
        g2, u2, xs2 = forward([x2, *s2])
        c_mid, xc_end = after((c_mid, xc_end), g2)
        x3, s3 = pick([c_mid, xc_end], [c_mid, xc_end])
        t2 = after(t2, x3, d1)
        f2, d2 = backward([c2, *t2], g2, u2)
        cc_end = after(cc_end, f2)
        c3, t3 = pick([c_mid, xc_end], (), [c_mid, cc_end])
        s3 = after(s3, c3)
        g3, u3, xs3 = forward([x3, *s3])
        t3 = after(t3, xs2, d2, xs3)
        f3, d3 = backward([c3, *t3], g3, u3)

        n = ff // n_dp

        def to_core(yy):
            return over_core(down_part(yy * NC + (1 - c_arr), hidden, cot_rows, n)[0])

        sent = [to_core(y_arr ^ k) for k in range(1, ny)]
        own_recv = to_core(y_arr)
        landed, totals = [], []
        for k in range(1, ny):
            recv = sent[k - 1]
            (total,) = down_part((y_arr ^ k) * NC + c_arr, hidden, cot_rows, n, [[after(recv, own_recv)]])
            landed.append([over_y(total, k)])
            totals.append(total)

        m = half // NC
        if m % LANES == 0:
            ds[0] = after(ds[0], totals)
            recv = [over_core(v) for v in both_part(1 - c_arr, xs, ds, m)]
            grad_gate, grad_up = both_part(c_arr, xs, ds, m, recv)
        else:
            x_all = jnp.concatenate(xs, axis=0)
            d_all = jnp.concatenate(ds, axis=0)

            def part(c):
                return contract_rows(lax.dynamic_slice_in_dim(x_all, c * m, m, 1), d_all)

            recv = over_core(part(1 - c_arr[0]).astype(BF16))
            total = (part(c_arr[0]) + recv.astype(F32)).astype(BF16)
            grad_gate, grad_up = total[:, :ff], total[:, ff:]

        (kept,) = down_part(
            y_arr * NC + c_arr, hidden, cot_rows, n, [[own_recv]], dtype=F32
        )
        landed = after(landed, kept, grad_up)
        for (part,) in landed:
            kept = kept + part.astype(F32)
        grad_down = kept.astype(BF16)
        return grad_gate[None], grad_up[None], grad_down[None]

    return per_device


def solution(mesh):
    in_specs = (
        P(("dp", "expert"), None),
        P(("dp", "expert"), None),
        P(("dp", "expert"), None),
        P(("dp", "expert"), None),
        P(),
        P("expert", None, None),
        P("expert", None, None),
        P("expert", None, None),
    )
    out_specs = (P("expert", "dp", None), P("expert", "dp", None), P("expert", "dp", None))
    per_device = make_per_device(mesh.shape["dp"], mesh.shape["expert"])
    return jax.shard_map(
        per_device, mesh=mesh, in_specs=in_specs, out_specs=out_specs, check_vma=False
    )
```

```python
import functools

import jax
import jax.numpy as jnp
from jax import lax
from jax.experimental import pallas as pl
from jax.experimental.pallas import tpu as pltpu
from jax.sharding import PartitionSpec as P

NZ = 4
NC = 2
F32, BF16 = jnp.float32, jnp.bfloat16
COST = pl.CostEstimate(flops=3000000000, bytes_accessed=1000, transcendentals=0)


LANES = 128


def params(mib):
    return pltpu.CompilerParams(vmem_limit_bytes=mib << 20)


def contract_rows(left, right):
    return lax.dot_general(left, right, (((0,), (0,)), ((), ())), preferred_element_type=F32)


def after(values, *deps):
    return lax.optimization_barrier((values, deps))[0]


def pack_kernel(routes_ref, gain_ref, tok_ref, cot_ref, out_ref):
    top = routes_ref.shape[0]
    toks, width = tok_ref.shape
    g = gain_ref[...]
    high = g.astype(BF16)
    g = g - high.astype(F32)
    mid = g.astype(BF16)
    low = (g - mid.astype(F32)).astype(BF16)
    rows = [routes_ref[...].astype(F32), high.astype(F32), mid.astype(F32), low.astype(F32)]
    total = jnp.zeros((toks, LANES), F32)
    for i, r in enumerate(rows):
        row = lax.broadcasted_iota(jnp.int32, (top, LANES), 0)
        col = lax.broadcasted_iota(jnp.int32, (top, LANES), 1)
        place = jnp.where(col == row + i * top, 1.0, 0.0).astype(BF16)
        total = total + contract_rows(r.astype(BF16), place)
    out_ref[:toks, :width] = tok_ref[...]
    out_ref[:toks, width:] = total.astype(BF16)
    out_ref[toks:, :width] = cot_ref[...]
    out_ref[toks:, width:] = jnp.zeros((toks, LANES), BF16)


def pack(tokens, cotangent, routes, gain):
    toks, width = tokens.shape
    return pl.pallas_call(
        pack_kernel,
        in_specs=[pl.BlockSpec(memory_space=pltpu.VMEM)] * 4,
        out_specs=pl.BlockSpec(memory_space=pltpu.VMEM),
        out_shape=jax.ShapeDtypeStruct((2 * toks, width + LANES), BF16),
        compiler_params=params(8),
        cost_estimate=COST,
        name="pack",
    )(routes.T, gain.T, tokens, cotangent)


def added(refs):
    value = refs[0][...]
    for r in refs[1:]:
        value = value + r[...]
    return value


def pick_kernel(ids_ref, *refs, nx, top, n_meta, n_x, n_c):
    meta_refs, refs = refs[:n_meta], refs[n_meta:]
    x_refs, c_refs, refs = refs[:n_x], refs[n_x : n_x + n_c], refs[n_x + n_c :]
    kinds = (1 if n_x else 0) + (1 if n_c else 0)
    own_refs, send_refs = refs[:kinds], refs[kinds : kinds + nx - 1]
    pick_ref, gain_ref = refs[-2:]
    cap, toks = pick_ref.shape[1:]

    @pl.when(pl.program_id(0) == 0)
    def _():
        row = lax.broadcasted_iota(jnp.int32, (4 * top, LANES), 0)
        col = lax.broadcasted_iota(jnp.int32, (4 * top, LANES), 1)
        place = jnp.where(col == row, 1.0, 0.0).astype(BF16)
        meta = lax.dot_general(
            place, added(meta_refs), (((1,), (1,)), ((), ())), preferred_element_type=F32
        )
        r = meta[0:top]
        g = (meta[top : 2 * top] + meta[2 * top : 3 * top]) + meta[3 * top :]
        row = lax.broadcasted_iota(jnp.int32, (toks, toks), 0)
        col = lax.broadcasted_iota(jnp.int32, (toks, toks), 1)
        before = jnp.where(row < col, 1.0, 0.0).astype(BF16)
        place = lax.broadcasted_iota(jnp.int32, (cap, toks), 0).astype(F32)
        for k in range(nx):
            named = r == ids_ref[0, k].astype(F32)
            alive = ids_ref[1, k].astype(F32)
            match = jnp.sum(jnp.where(named, 1.0, 0.0), axis=0, keepdims=True) * alive
            gain_t = jnp.sum(jnp.where(named, g, 0.0), axis=0, keepdims=True)
            wide = jnp.broadcast_to(match, (8, toks)).astype(BF16)
            pos = jnp.dot(wide, before, preferred_element_type=F32)[0:1]
            pick = jnp.where(place == pos, jnp.broadcast_to(match, (cap, toks)), 0.0)
            pick_ref[k] = pick.astype(BF16)
            if n_c:
                gain_ref[k] = jnp.sum(pick * gain_t, axis=1, keepdims=True)

    for i, (block_refs, weighted) in enumerate(
        ([(x_refs, False)] if n_x else []) + ([(c_refs, True)] if n_c else [])
    ):
        block = added(block_refs)
        for k in range(nx):
            sel = jnp.dot(pick_ref[k], block, preferred_element_type=F32)
            if weighted:
                sel = gain_ref[k] * sel
            if k == 0:
                own_refs[i][...] = sel.astype(BF16)
            else:
                send_refs[k - 1][i * cap : (i + 1) * cap, :] = sel.astype(BF16)


def pick_rows(ids, metas, xs, cs, nx, cap, top, width, toks):
    tile = width // 4
    kinds = (1 if xs else 0) + (1 if cs else 0)
    own, *sends = pl.pallas_call(
        functools.partial(
            pick_kernel, nx=nx, top=top, n_meta=len(metas), n_x=len(xs), n_c=len(cs)
        ),
        grid=(width // tile,),
        in_specs=[pl.BlockSpec(memory_space=pltpu.SMEM)]
        + [pl.BlockSpec((toks, LANES), lambda j: (0, width // LANES))] * len(metas)
        + [pl.BlockSpec((toks, tile), lambda j: (0, j))] * len(xs)
        + [
            pl.BlockSpec((toks, tile), lambda j, at=v.shape[0] // toks - 1: (at, j)) for v in cs
        ],
        out_specs=[pl.BlockSpec((cap, tile), lambda j: (0, j))] * kinds
        + [pl.BlockSpec((kinds * cap, tile), lambda j: (0, j))] * (nx - 1),
        out_shape=[jax.ShapeDtypeStruct((cap, width), BF16)] * kinds
        + [jax.ShapeDtypeStruct((kinds * cap, width), BF16)] * (nx - 1),
        scratch_shapes=[pltpu.VMEM((nx, cap, toks), BF16), pltpu.VMEM((nx, cap, 1), F32)],
        compiler_params=params(6),
        cost_estimate=COST,
        name="pick",
    )(ids, *metas, *xs, *cs)
    return own, sends


def whole(count):
    return [pl.BlockSpec(memory_space=pltpu.VMEM)] * count


def gate_up_kernel(y_ref, *refs, parts, ny):
    rows_in, (wg_ref, wu_ref) = refs[:parts], refs[parts : parts + 2]
    gate_ref, up_ref, *splits = refs[parts + 2 : parts + 4 + ny]
    joined = refs[parts + 4 + ny]
    cap = rows_in[0].shape[0]
    for k in range(parts):
        joined[k * cap : (k + 1) * cap, :] = rows_in[k][...]
    half = joined.shape[1] // ny
    for k in range(ny):
        begin = pl.multiple_of((y_ref[0] ^ k) * half, LANES)
        splits[k][...] = joined[:, pl.ds(begin, half)]
    x = joined[...]
    gate_ref[...] = jnp.dot(x, wg_ref[0], preferred_element_type=F32)
    up_ref[...] = jnp.dot(x, wu_ref[0], preferred_element_type=F32)


def gate_up(y, parts, w_gate, w_up, ny):
    cap, width = parts[0].shape
    ff = w_gate.shape[2]
    rows = cap * len(parts)
    return pl.pallas_call(
        functools.partial(gate_up_kernel, parts=len(parts), ny=ny),
        in_specs=[pl.BlockSpec(memory_space=pltpu.SMEM)] + whole(len(parts) + 2),
        out_specs=whole(2 + ny),
        out_shape=[jax.ShapeDtypeStruct((rows, ff), F32)] * 2
        + [jax.ShapeDtypeStruct((rows, width // ny), BF16)] * ny,
        scratch_shapes=[pltpu.VMEM((rows, width), BF16)],
        compiler_params=params(10),
        cost_estimate=COST,
        name="gate_up",
    )(y, *parts, w_gate, w_up)


def back_kernel(*refs, parts):
    rows_in, (wd_ref, gate_ref, up_ref) = refs[:parts], refs[parts : parts + 3]
    d_ref, hid_ref, cot_ref = refs[parts + 3 :]
    cap = rows_in[0].shape[0]
    ff = gate_ref.shape[1]
    for k in range(parts):
        cot_ref[k * cap : (k + 1) * cap, :] = rows_in[k][...]
    total = lax.dot_general(
        cot_ref[...], wd_ref[0], (((1,), (1,)), ((), ())), preferred_element_type=F32
    )
    gate, up = gate_ref[...], up_ref[...]
    sig = jax.nn.sigmoid(gate)
    act = gate * sig
    hid_ref[...] = (act * up).astype(BF16)
    d_ref[:, :ff] = (total * up * sig * (1.0 + gate * (1.0 - sig))).astype(BF16)
    d_ref[:, ff:] = (total * act).astype(BF16)


def back(parts, w_down, gate, up):
    width = parts[0].shape[1]
    rows, ff = gate.shape
    n = len(parts)
    return pl.pallas_call(
        functools.partial(back_kernel, parts=n),
        in_specs=whole(n + 3),
        out_specs=whole(3),
        out_shape=[
            jax.ShapeDtypeStruct((rows, 2 * ff), BF16),
            jax.ShapeDtypeStruct((rows, ff), BF16),
            jax.ShapeDtypeStruct((rows, width), BF16),
        ],
        compiler_params=params(10),
        cost_estimate=COST,
        name="back",
    )(*parts, w_down, gate, up)


def sends_kernel(s_ref, *refs, pieces):
    lefts, cots, refs = refs[: 2 * pieces], refs[2 * pieces : 3 * pieces], refs[3 * pieces :]
    outs, (left, right) = refs[:2], refs[2:]
    rows = cots[0].shape[0]
    for k in range(pieces):
        right[k * rows : (k + 1) * rows, :] = cots[k][...]
    for i in range(2):
        for k in range(pieces):
            left[k * rows : (k + 1) * rows, :] = lefts[i * pieces + k][...]
        outs[i][...] = contract_rows(left[...], right[...]).astype(BF16)


def down_sends(indices, hidden, cot, n):
    rows, width = cot[0].shape
    m = len(cot)
    tile = width // 4
    return pl.pallas_call(
        functools.partial(sends_kernel, pieces=m),
        grid_spec=pltpu.PrefetchScalarGridSpec(
            num_scalar_prefetch=1,
            grid=(4,),
            in_specs=[
                pl.BlockSpec((rows, n), lambda j, s_ref, i=i: (0, s_ref[i]))
                for i in range(2)
                for _ in range(m)
            ]
            + [pl.BlockSpec((rows, tile), lambda j, s_ref: (0, j))] * m,
            out_specs=[pl.BlockSpec((n, tile), lambda j, s_ref: (0, j))] * 2,
            scratch_shapes=[pltpu.VMEM((m * rows, n), BF16), pltpu.VMEM((m * rows, tile), BF16)],
        ),
        out_shape=[jax.ShapeDtypeStruct((n, width), BF16)] * 2,
        compiler_params=params(12),
        cost_estimate=COST,
        name="down_sends",
    )(indices, *hidden, *hidden, *cot)


def down_kernel(s_ref, *refs, pieces, ins, outs):
    hids, cots, refs = refs[:pieces], refs[pieces : 2 * pieces], refs[2 * pieces :]
    in_refs, out_refs, (left, right, acc) = refs[: len(ins)], refs[len(ins) : -3], refs[-3:]
    j = pl.program_id(0)
    rows = hids[0].shape[0]
    for k in range(pieces):
        left[k * rows : (k + 1) * rows, :] = hids[k][...]
        right[k * rows : (k + 1) * rows, :] = cots[k][...]
    acc[...] = contract_rows(left[...], right[...])
    for (begin, size), ref in zip(ins, in_refs):

        @pl.when((j >= begin) & (j < begin + size))
        def _(ref=ref):
            acc[...] += ref[...].astype(F32)

    for (begin, size), ref in zip(outs, out_refs):

        @pl.when((j >= begin) & (j < begin + size))
        def _(ref=ref):
            ref[...] = acc[...].astype(ref.dtype)


def down_part(index, hidden, cot, n, arrived=(), outs=(4,), dtype=BF16):
    rows, width = cot[0].shape
    m = len(cot)
    steps = 4
    tile = width // steps

    def ranges(sizes):
        return [(sum(sizes[:i]), size) for i, size in enumerate(sizes)]

    def chunk(begin, size):
        return pl.BlockSpec(
            (n, tile), lambda j, s_ref: (0, jnp.minimum(jnp.maximum(j - begin, 0), size - 1))
        )

    ins = [r for a in arrived for r in ranges([v.shape[1] // tile for v in a])]
    outs = ranges(outs)
    return pl.pallas_call(
        functools.partial(down_kernel, pieces=m, ins=ins, outs=outs),
        grid_spec=pltpu.PrefetchScalarGridSpec(
            num_scalar_prefetch=1,
            grid=(steps,),
            in_specs=[pl.BlockSpec((rows, n), lambda j, s_ref: (0, s_ref[0]))] * m
            + [pl.BlockSpec((rows, tile), lambda j, s_ref: (0, j))] * m
            + [chunk(*r) for r in ins],
            out_specs=[chunk(*r) for r in outs],
            scratch_shapes=[
                pltpu.VMEM((m * rows, n), BF16),
                pltpu.VMEM((m * rows, tile), BF16),
                pltpu.VMEM((n, tile), F32),
            ],
        ),
        out_shape=[jax.ShapeDtypeStruct((n, tile * size), dtype) for _, size in outs],
        compiler_params=params(9),
        cost_estimate=COST,
        name="down_part",
    )(index, *hidden, *cot, *[piece for a in arrived for piece in a])


def both_kernel(c_ref, *refs, pieces, add):
    xs, ds = refs[:pieces], refs[pieces : 2 * pieces]
    rest = refs[2 * pieces :]
    got, outs, (left, right, acc) = rest[:add], rest[add:-3], rest[-3:]
    rows = xs[0].shape[0]
    j = pl.program_id(0)

    @pl.when(j == 0)
    def _():
        for i in range(pieces):
            left[i * rows : (i + 1) * rows, :] = xs[i][...]

    for i in range(pieces):
        right[i * rows : (i + 1) * rows, :] = ds[i][...]
    acc[...] = contract_rows(left[...], right[...])
    for w, ref in enumerate(got):

        @pl.when(j == w)
        def _(ref=ref):
            acc[...] += ref[...].astype(F32)

    for w, out in enumerate(outs):

        @pl.when(j * len(outs) // pl.num_programs(0) == w)
        def _(w=w, out=out):
            total = acc[...]
            out[...] = total.astype(BF16)


def both_part(index, xs, ds, n, arrived=()):
    rows, ff2 = ds[0].shape
    steps, tile = 4, ff2 // 4
    m = len(xs)
    add = len(arrived)
    outs = 2 if add else steps
    per = steps // outs

    return pl.pallas_call(
        functools.partial(both_kernel, pieces=m, add=add),
        grid_spec=pltpu.PrefetchScalarGridSpec(
            num_scalar_prefetch=1,
            grid=(steps,),
            in_specs=[pl.BlockSpec((rows, n), lambda j, c_ref: (0, c_ref[0]))] * m
            + [pl.BlockSpec((rows, tile), lambda j, c_ref: (0, j))] * m
            + [pl.BlockSpec((n, tile), lambda j, c_ref: (0, 0))] * add,
            out_specs=[
                pl.BlockSpec(
                    (n, tile),
                    lambda j, c_ref, w=w: (0, jnp.minimum(jnp.maximum(j - w * per, 0), per - 1)),
                )
                for w in range(outs)
            ],
            scratch_shapes=[
                pltpu.VMEM((m * rows, n), BF16),
                pltpu.VMEM((m * rows, tile), BF16),
                pltpu.VMEM((n, tile), F32),
            ],
        ),
        out_shape=[jax.ShapeDtypeStruct((n, ff2 // outs), BF16)] * outs,
        compiler_params=params(22),
        cost_estimate=COST,
        name="both_part",
    )(index, *xs, *ds, *arrived)


def make_per_device(n_dp, n_expert):
    nx = n_expert // NZ
    ny = n_dp // NC

    def ex(z, x):
        return z * nx + x

    def zpairs(moves):
        return [(ex(a, x), ex(b, x)) for a, b in moves for x in range(nx)]

    ends_first = zpairs([(0, 1), (1, 0), (2, 3), (3, 2)])
    middle = zpairs([(1, 2), (2, 1)])
    outward = zpairs([(1, 0), (2, 3)])

    def hop1(block):
        return lax.ppermute(block, "expert", ends_first), lax.ppermute(block, "expert", middle)

    def hop2(a, c_mid):
        return lax.ppermute(c_mid, "expert", outward), lax.ppermute(a, "expert", middle)

    def hop3(b_mid):
        return lax.ppermute(b_mid, "expert", outward)

    def over_x(sends):
        out = []
        for k in range(1, nx):
            pairs = [(ex(z, x), ex(z, x ^ k)) for z in range(NZ) for x in range(nx)]
            out.append(lax.ppermute(sends[k - 1], "expert", pairs))
        return out

    core_pairs = [(y * NC + c, y * NC + 1 - c) for y in range(ny) for c in range(NC)]

    def over_core(value):
        return lax.ppermute(value, "dp", core_pairs)

    def over_y(value, k):
        return lax.ppermute(
            value, "dp", [(y * NC + c, (y ^ k) * NC + c) for y in range(ny) for c in range(NC)]
        )

    def per_device(tokens, cotangent, routes, route_gain, expert_alive, w_gate, w_up, w_down):
        tok_count, width = tokens.shape
        top = routes.shape[1]
        experts_all = expert_alive.shape[0]
        cap = tok_count * top * 5 // (4 * experts_all)
        ff = w_gate.shape[2]
        half = width // ny
        me = lax.axis_index("expert")
        z, x = me // nx, me % nx
        d = lax.axis_index("dp")
        y_arr = (d // NC).astype(jnp.int32)[None]
        c_arr = (d % NC).astype(jnp.int32)[None]

        own = pack(tokens, cotangent, routes, route_gain)
        a, c_mid = hop1(own)

        own_ids = z * nx + (x ^ jnp.arange(nx, dtype=jnp.int32))
        alive = jnp.sum(
            jnp.where(
                own_ids[:, None] == jnp.arange(experts_all)[None, :], expert_alive[None, :], 0
            ),
            axis=1,
        )
        ids = jnp.stack([own_ids, alive.astype(jnp.int32)])

        def pick(metas, xs=(), cs=()):
            own, sends = pick_rows(ids, metas, xs, cs, nx, cap, top, width, tok_count)
            return own, over_x(sends)

        xs, ds, hidden, cot_rows = [], [], [], []

        def spread(pieces, values):
            got = [over_y(values[k], k) for k in range(1, ny)]
            pieces += [values[0], *got]
            return got

        def forward(parts):
            gate, up, *splits = gate_up(y_arr, parts, w_gate, w_up, ny)
            return gate, up, spread(xs, splits)

        def backward(parts, gate, up):
            both, hid, cot = back(parts, w_down, gate, up)
            hidden.append(hid)
            cot_rows.append(cot)
            return both, spread(ds, [both] * ny)

        x0, s0 = pick([own], [own])
        c0, t0 = pick([own], (), [after(own, x0)])
        g0, u0, xs0 = forward([x0, *s0])
        f0, d0 = backward([c0, *t0], g0, u0)
        a, c_mid = after((a, c_mid), f0)
        b_end, b_mid = hop2(a, c_mid)
        x1, s1 = pick([a], [a])
        c1, t1 = pick([a], (), [after(a, x1)])
        s1 = after(s1, c1, xs0)
        g1, u1, xs1 = forward([x1, *s1])
        t1 = after(t1, d0)
        f1, d1 = backward([c1, *t1], g1, u1)
        xc_end = hop3(b_mid[:tok_count])
        cc_end = hop3(b_mid[tok_count:, :width])
        b_end, b_mid = after((b_end, b_mid), f1)
        x2, s2 = pick([b_end, b_mid], [b_end, b_mid])
        c2, t2 = pick([b_end, b_mid], (), after([b_end, b_mid], x2))
        s2 = after(s2, c2, xs1)
        g2, u2, xs2 = forward([x2, *s2])
        c_mid, xc_end = after((c_mid, xc_end), g2)
        x3, s3 = pick([c_mid, xc_end], [c_mid, xc_end])
        t2 = after(t2, x3, d1)
        f2, d2 = backward([c2, *t2], g2, u2)
        cc_end = after(cc_end, f2)
        c3, t3 = pick([c_mid, xc_end], (), [c_mid, cc_end])
        s3 = after(s3, c3)
        g3, u3, xs3 = forward([x3, *s3])
        t3 = after(t3, xs2, d2)
        f3, d3 = backward([c3, *t3], g3, u3)

        n = ff // n_dp
        hidden = after(hidden, xs3)

        def to_core(yy):
            return over_core(down_part(yy * NC + (1 - c_arr), hidden, cot_rows, n)[0])

        if ny == 2:
            other = jnp.concatenate([(y_arr ^ k) * NC + (1 - c_arr) for k in (1, 0)])
            first, second = down_sends(other, hidden, cot_rows, n)
            sent, own_recv = [over_core(first)], over_core(second)
        else:
            sent = [to_core(y_arr ^ k) for k in range(1, ny)]
            own_recv = to_core(y_arr)
        landed, totals = [], []
        for k in range(1, ny):
            recv = sent[k - 1]
            (total,) = down_part((y_arr ^ k) * NC + c_arr, hidden, cot_rows, n, [[after(recv, own_recv)]])
            landed.append([over_y(total, k)])
            totals.append(total)

        m = half // NC
        if m % LANES == 0:
            ds[0] = after(ds[0], totals)
            recv = [over_core(v) for v in both_part(1 - c_arr, xs, ds, m)]
            grad_gate, grad_up = both_part(c_arr, xs, ds, m, recv)
        else:
            x_all = jnp.concatenate(xs, axis=0)
            d_all = jnp.concatenate(ds, axis=0)

            def part(c):
                return contract_rows(lax.dynamic_slice_in_dim(x_all, c * m, m, 1), d_all)

            recv = over_core(part(1 - c_arr[0]).astype(BF16))
            total = (part(c_arr[0]) + recv.astype(F32)).astype(BF16)
            grad_gate, grad_up = total[:, :ff], total[:, ff:]

        (kept,) = down_part(
            y_arr * NC + c_arr, hidden, cot_rows, n, [[own_recv]], dtype=F32
        )
        landed = after(landed, kept, grad_up)
        for (part,) in landed:
            kept = kept + part.astype(F32)
        grad_down = kept.astype(BF16)
        return grad_gate[None], grad_up[None], grad_down[None]

    return per_device


def solution(mesh):
    in_specs = (
        P(("dp", "expert"), None),
        P(("dp", "expert"), None),
        P(("dp", "expert"), None),
        P(("dp", "expert"), None),
        P(),
        P("expert", None, None),
        P("expert", None, None),
        P("expert", None, None),
    )
    out_specs = (P("expert", "dp", None), P("expert", "dp", None), P("expert", "dp", None))
    per_device = make_per_device(mesh.shape["dp"], mesh.shape["expert"])
    return jax.shard_map(
        per_device, mesh=mesh, in_specs=in_specs, out_specs=out_specs, check_vma=False
    )
```

```python
import functools

import jax
import jax.numpy as jnp
from jax import lax
from jax.experimental import pallas as pl
from jax.experimental.pallas import tpu as pltpu
from jax.sharding import PartitionSpec as P

NZ = 4
NC = 2
F32, BF16 = jnp.float32, jnp.bfloat16
COST = pl.CostEstimate(flops=2000000000, bytes_accessed=1000, transcendentals=0)


LANES = 128


def params(mib):
    return pltpu.CompilerParams(vmem_limit_bytes=mib << 20)


def contract_rows(left, right):
    return lax.dot_general(left, right, (((0,), (0,)), ((), ())), preferred_element_type=F32)


def after(values, *deps):
    return lax.optimization_barrier((values, deps))[0]


def pack_kernel(routes_ref, gain_ref, tok_ref, cot_ref, out_ref):
    top = routes_ref.shape[0]
    toks, width = tok_ref.shape
    g = gain_ref[...]
    high = g.astype(BF16)
    g = g - high.astype(F32)
    mid = g.astype(BF16)
    low = (g - mid.astype(F32)).astype(BF16)
    rows = [routes_ref[...].astype(F32), high.astype(F32), mid.astype(F32), low.astype(F32)]
    total = jnp.zeros((toks, LANES), F32)
    for i, r in enumerate(rows):
        row = lax.broadcasted_iota(jnp.int32, (top, LANES), 0)
        col = lax.broadcasted_iota(jnp.int32, (top, LANES), 1)
        place = jnp.where(col == row + i * top, 1.0, 0.0).astype(BF16)
        total = total + contract_rows(r.astype(BF16), place)
    out_ref[:toks, :width] = tok_ref[...]
    out_ref[:toks, width:] = total.astype(BF16)
    out_ref[toks:, :width] = cot_ref[...]
    out_ref[toks:, width:] = jnp.zeros((toks, LANES), BF16)


def pack(tokens, cotangent, routes, gain):
    toks, width = tokens.shape
    return pl.pallas_call(
        pack_kernel,
        in_specs=[pl.BlockSpec(memory_space=pltpu.VMEM)] * 4,
        out_specs=pl.BlockSpec(memory_space=pltpu.VMEM),
        out_shape=jax.ShapeDtypeStruct((2 * toks, width + LANES), BF16),
        compiler_params=params(8),
        cost_estimate=COST,
        name="pack",
    )(routes.T, gain.T, tokens, cotangent)


def added(refs):
    value = refs[0][...]
    for r in refs[1:]:
        value = value + r[...]
    return value


def pick_kernel(ids_ref, *refs, nx, top, n_meta, n_x, n_c):
    meta_refs, refs = refs[:n_meta], refs[n_meta:]
    x_refs, c_refs, refs = refs[:n_x], refs[n_x : n_x + n_c], refs[n_x + n_c :]
    kinds = (1 if n_x else 0) + (1 if n_c else 0)
    own_refs, send_refs = refs[:kinds], refs[kinds : kinds + nx - 1]
    pick_ref, gain_ref = refs[-2:]
    cap, toks = pick_ref.shape[1:]

    @pl.when(pl.program_id(0) == 0)
    def _():
        row = lax.broadcasted_iota(jnp.int32, (4 * top, LANES), 0)
        col = lax.broadcasted_iota(jnp.int32, (4 * top, LANES), 1)
        place = jnp.where(col == row, 1.0, 0.0).astype(BF16)
        meta = lax.dot_general(
            place, added(meta_refs), (((1,), (1,)), ((), ())), preferred_element_type=F32
        )
        r = meta[0:top]
        g = (meta[top : 2 * top] + meta[2 * top : 3 * top]) + meta[3 * top :]
        row = lax.broadcasted_iota(jnp.int32, (toks, toks), 0)
        col = lax.broadcasted_iota(jnp.int32, (toks, toks), 1)
        before = jnp.where(row < col, 1.0, 0.0).astype(BF16)
        place = lax.broadcasted_iota(jnp.int32, (cap, toks), 0).astype(F32)
        for k in range(nx):
            named = r == ids_ref[0, k].astype(F32)
            alive = ids_ref[1, k].astype(F32)
            match = jnp.sum(jnp.where(named, 1.0, 0.0), axis=0, keepdims=True) * alive
            gain_t = jnp.sum(jnp.where(named, g, 0.0), axis=0, keepdims=True)
            wide = jnp.broadcast_to(match, (8, toks)).astype(BF16)
            pos = jnp.dot(wide, before, preferred_element_type=F32)[0:1]
            pick = jnp.where(place == pos, jnp.broadcast_to(match, (cap, toks)), 0.0)
            pick_ref[k] = pick.astype(BF16)
            if n_c:
                gain_ref[k] = jnp.sum(pick * gain_t, axis=1, keepdims=True)

    for i, (block_refs, weighted) in enumerate(
        ([(x_refs, False)] if n_x else []) + ([(c_refs, True)] if n_c else [])
    ):
        block = added(block_refs)
        for k in range(nx):
            sel = jnp.dot(pick_ref[k], block, preferred_element_type=F32)
            if weighted:
                sel = gain_ref[k] * sel
            if k == 0:
                own_refs[i][...] = sel.astype(BF16)
            else:
                send_refs[k - 1][i * cap : (i + 1) * cap, :] = sel.astype(BF16)


def pick_rows(ids, metas, xs, cs, nx, cap, top, width, toks):
    tile = width // 4
    kinds = (1 if xs else 0) + (1 if cs else 0)
    own, *sends = pl.pallas_call(
        functools.partial(
            pick_kernel, nx=nx, top=top, n_meta=len(metas), n_x=len(xs), n_c=len(cs)
        ),
        grid=(width // tile,),
        in_specs=[pl.BlockSpec(memory_space=pltpu.SMEM)]
        + [pl.BlockSpec((toks, LANES), lambda j: (0, width // LANES))] * len(metas)
        + [pl.BlockSpec((toks, tile), lambda j: (0, j))] * len(xs)
        + [
            pl.BlockSpec((toks, tile), lambda j, at=v.shape[0] // toks - 1: (at, j)) for v in cs
        ],
        out_specs=[pl.BlockSpec((cap, tile), lambda j: (0, j))] * kinds
        + [pl.BlockSpec((kinds * cap, tile), lambda j: (0, j))] * (nx - 1),
        out_shape=[jax.ShapeDtypeStruct((cap, width), BF16)] * kinds
        + [jax.ShapeDtypeStruct((kinds * cap, width), BF16)] * (nx - 1),
        scratch_shapes=[pltpu.VMEM((nx, cap, toks), BF16), pltpu.VMEM((nx, cap, 1), F32)],
        compiler_params=params(6),
        cost_estimate=COST,
        name="pick",
    )(ids, *metas, *xs, *cs)
    return own, sends


def whole(count):
    return [pl.BlockSpec(memory_space=pltpu.VMEM)] * count


def gate_up_kernel(y_ref, *refs, parts, ny):
    rows_in, (wg_ref, wu_ref) = refs[:parts], refs[parts : parts + 2]
    gate_ref, up_ref, *splits = refs[parts + 2 : parts + 4 + ny]
    joined = refs[parts + 4 + ny]
    cap = rows_in[0].shape[0]
    for k in range(parts):
        joined[k * cap : (k + 1) * cap, :] = rows_in[k][...]
    half = joined.shape[1] // ny
    for k in range(ny):
        begin = pl.multiple_of((y_ref[0] ^ k) * half, LANES)
        splits[k][...] = joined[:, pl.ds(begin, half)]
    x = joined[...]
    gate_ref[...] = jnp.dot(x, wg_ref[0], preferred_element_type=F32)
    up_ref[...] = jnp.dot(x, wu_ref[0], preferred_element_type=F32)


def gate_up(y, parts, w_gate, w_up, ny):
    cap, width = parts[0].shape
    ff = w_gate.shape[2]
    rows = cap * len(parts)
    return pl.pallas_call(
        functools.partial(gate_up_kernel, parts=len(parts), ny=ny),
        in_specs=[pl.BlockSpec(memory_space=pltpu.SMEM)] + whole(len(parts) + 2),
        out_specs=whole(2 + ny),
        out_shape=[jax.ShapeDtypeStruct((rows, ff), F32)] * 2
        + [jax.ShapeDtypeStruct((rows, width // ny), BF16)] * ny,
        scratch_shapes=[pltpu.VMEM((rows, width), BF16)],
        compiler_params=params(10),
        cost_estimate=COST,
        name="gate_up",
    )(y, *parts, w_gate, w_up)


def back_kernel(*refs, parts):
    rows_in, (wd_ref, gate_ref, up_ref) = refs[:parts], refs[parts : parts + 3]
    d_ref, hid_ref, cot_ref = refs[parts + 3 :]
    cap = rows_in[0].shape[0]
    ff = gate_ref.shape[1]
    for k in range(parts):
        cot_ref[k * cap : (k + 1) * cap, :] = rows_in[k][...]
    total = lax.dot_general(
        cot_ref[...], wd_ref[0], (((1,), (1,)), ((), ())), preferred_element_type=F32
    )
    gate, up = gate_ref[...], up_ref[...]
    sig = jax.nn.sigmoid(gate)
    act = gate * sig
    hid_ref[...] = (act * up).astype(BF16)
    d_ref[:, :ff] = (total * up * sig * (1.0 + gate * (1.0 - sig))).astype(BF16)
    d_ref[:, ff:] = (total * act).astype(BF16)


def back(parts, w_down, gate, up):
    width = parts[0].shape[1]
    rows, ff = gate.shape
    n = len(parts)
    return pl.pallas_call(
        functools.partial(back_kernel, parts=n),
        in_specs=whole(n + 3),
        out_specs=whole(3),
        out_shape=[
            jax.ShapeDtypeStruct((rows, 2 * ff), BF16),
            jax.ShapeDtypeStruct((rows, ff), BF16),
            jax.ShapeDtypeStruct((rows, width), BF16),
        ],
        compiler_params=params(10),
        cost_estimate=COST,
        name="back",
    )(*parts, w_down, gate, up)


def sends_kernel(s_ref, *refs, pieces):
    lefts, cots, refs = refs[: 2 * pieces], refs[2 * pieces : 3 * pieces], refs[3 * pieces :]
    outs, (left, right) = refs[:2], refs[2:]
    rows = cots[0].shape[0]
    for k in range(pieces):
        right[k * rows : (k + 1) * rows, :] = cots[k][...]
    for i in range(2):
        for k in range(pieces):
            left[k * rows : (k + 1) * rows, :] = lefts[i * pieces + k][...]
        outs[i][...] = contract_rows(left[...], right[...]).astype(BF16)


def down_sends(indices, hidden, cot, n):
    rows, width = cot[0].shape
    m = len(cot)
    tile = width // 4
    return pl.pallas_call(
        functools.partial(sends_kernel, pieces=m),
        grid_spec=pltpu.PrefetchScalarGridSpec(
            num_scalar_prefetch=1,
            grid=(4,),
            in_specs=[
                pl.BlockSpec((rows, n), lambda j, s_ref, i=i: (0, s_ref[i]))
                for i in range(2)
                for _ in range(m)
            ]
            + [pl.BlockSpec((rows, tile), lambda j, s_ref: (0, j))] * m,
            out_specs=[pl.BlockSpec((n, tile), lambda j, s_ref: (0, j))] * 2,
            scratch_shapes=[pltpu.VMEM((m * rows, n), BF16), pltpu.VMEM((m * rows, tile), BF16)],
        ),
        out_shape=[jax.ShapeDtypeStruct((n, width), BF16)] * 2,
        compiler_params=params(12),
        cost_estimate=COST,
        name="down_sends",
    )(indices, *hidden, *hidden, *cot)


def down_kernel(s_ref, *refs, pieces, ins, outs):
    hids, cots, refs = refs[:pieces], refs[pieces : 2 * pieces], refs[2 * pieces :]
    in_refs, out_refs, (left, right, acc) = refs[: len(ins)], refs[len(ins) : -3], refs[-3:]
    j = pl.program_id(0)
    rows = hids[0].shape[0]
    for k in range(pieces):
        left[k * rows : (k + 1) * rows, :] = hids[k][...]
        right[k * rows : (k + 1) * rows, :] = cots[k][...]
    acc[...] = contract_rows(left[...], right[...])
    for (begin, size), ref in zip(ins, in_refs):

        @pl.when((j >= begin) & (j < begin + size))
        def _(ref=ref):
            acc[...] += ref[...].astype(F32)

    for (begin, size), ref in zip(outs, out_refs):

        @pl.when((j >= begin) & (j < begin + size))
        def _(ref=ref):
            ref[...] = acc[...].astype(ref.dtype)


def down_part(index, hidden, cot, n, arrived=(), outs=(4,), dtype=BF16):
    rows, width = cot[0].shape
    m = len(cot)
    steps = 4
    tile = width // steps

    def ranges(sizes):
        return [(sum(sizes[:i]), size) for i, size in enumerate(sizes)]

    def chunk(begin, size):
        return pl.BlockSpec(
            (n, tile), lambda j, s_ref: (0, jnp.minimum(jnp.maximum(j - begin, 0), size - 1))
        )

    ins = [r for a in arrived for r in ranges([v.shape[1] // tile for v in a])]
    outs = ranges(outs)
    return pl.pallas_call(
        functools.partial(down_kernel, pieces=m, ins=ins, outs=outs),
        grid_spec=pltpu.PrefetchScalarGridSpec(
            num_scalar_prefetch=1,
            grid=(steps,),
            in_specs=[pl.BlockSpec((rows, n), lambda j, s_ref: (0, s_ref[0]))] * m
            + [pl.BlockSpec((rows, tile), lambda j, s_ref: (0, j))] * m
            + [chunk(*r) for r in ins],
            out_specs=[chunk(*r) for r in outs],
            scratch_shapes=[
                pltpu.VMEM((m * rows, n), BF16),
                pltpu.VMEM((m * rows, tile), BF16),
                pltpu.VMEM((n, tile), F32),
            ],
        ),
        out_shape=[jax.ShapeDtypeStruct((n, tile * size), dtype) for _, size in outs],
        compiler_params=params(9),
        cost_estimate=COST,
        name="down_part",
    )(index, *hidden, *cot, *[piece for a in arrived for piece in a])


def both_kernel(c_ref, *refs, pieces, add):
    xs, ds = refs[:pieces], refs[pieces : 2 * pieces]
    rest = refs[2 * pieces :]
    got, outs, (left, right, acc) = rest[:add], rest[add:-3], rest[-3:]
    rows = xs[0].shape[0]
    j = pl.program_id(0)

    @pl.when(j == 0)
    def _():
        for i in range(pieces):
            left[i * rows : (i + 1) * rows, :] = xs[i][...]

    for i in range(pieces):
        right[i * rows : (i + 1) * rows, :] = ds[i][...]
    acc[...] = contract_rows(left[...], right[...])
    for w, ref in enumerate(got):

        @pl.when(j == w)
        def _(ref=ref):
            acc[...] += ref[...].astype(F32)

    for w, out in enumerate(outs):

        @pl.when(j * len(outs) // pl.num_programs(0) == w)
        def _(w=w, out=out):
            total = acc[...]
            out[...] = total.astype(BF16)


def both_part(index, xs, ds, n, arrived=()):
    rows, ff2 = ds[0].shape
    steps, tile = 4, ff2 // 4
    m = len(xs)
    add = len(arrived)
    outs = 2 if add else steps
    per = steps // outs

    return pl.pallas_call(
        functools.partial(both_kernel, pieces=m, add=add),
        grid_spec=pltpu.PrefetchScalarGridSpec(
            num_scalar_prefetch=1,
            grid=(steps,),
            in_specs=[pl.BlockSpec((rows, n), lambda j, c_ref: (0, c_ref[0]))] * m
            + [pl.BlockSpec((rows, tile), lambda j, c_ref: (0, j))] * m
            + [pl.BlockSpec((n, tile), lambda j, c_ref: (0, 0))] * add,
            out_specs=[
                pl.BlockSpec(
                    (n, tile),
                    lambda j, c_ref, w=w: (0, jnp.minimum(jnp.maximum(j - w * per, 0), per - 1)),
                )
                for w in range(outs)
            ],
            scratch_shapes=[
                pltpu.VMEM((m * rows, n), BF16),
                pltpu.VMEM((m * rows, tile), BF16),
                pltpu.VMEM((n, tile), F32),
            ],
        ),
        out_shape=[jax.ShapeDtypeStruct((n, ff2 // outs), BF16)] * outs,
        compiler_params=params(22),
        cost_estimate=COST,
        name="both_part",
    )(index, *xs, *ds, *arrived)


def make_per_device(n_dp, n_expert):
    nx = n_expert // NZ
    ny = n_dp // NC

    def ex(z, x):
        return z * nx + x

    def zpairs(moves):
        return [(ex(a, x), ex(b, x)) for a, b in moves for x in range(nx)]

    ends_first = zpairs([(0, 1), (1, 0), (2, 3), (3, 2)])
    middle = zpairs([(1, 2), (2, 1)])
    outward = zpairs([(1, 0), (2, 3)])

    def hop1(block):
        return lax.ppermute(block, "expert", ends_first), lax.ppermute(block, "expert", middle)

    def hop2(a, c_mid):
        return lax.ppermute(c_mid, "expert", outward), lax.ppermute(a, "expert", middle)

    def hop3(b_mid):
        return lax.ppermute(b_mid, "expert", outward)

    def over_x(sends):
        out = []
        for k in range(1, nx):
            pairs = [(ex(z, x), ex(z, x ^ k)) for z in range(NZ) for x in range(nx)]
            out.append(lax.ppermute(sends[k - 1], "expert", pairs))
        return out

    core_pairs = [(y * NC + c, y * NC + 1 - c) for y in range(ny) for c in range(NC)]

    def over_core(value):
        return lax.ppermute(value, "dp", core_pairs)

    def over_y(value, k):
        return lax.ppermute(
            value, "dp", [(y * NC + c, (y ^ k) * NC + c) for y in range(ny) for c in range(NC)]
        )

    def per_device(tokens, cotangent, routes, route_gain, expert_alive, w_gate, w_up, w_down):
        tok_count, width = tokens.shape
        top = routes.shape[1]
        experts_all = expert_alive.shape[0]
        cap = tok_count * top * 5 // (4 * experts_all)
        ff = w_gate.shape[2]
        half = width // ny
        me = lax.axis_index("expert")
        z, x = me // nx, me % nx
        d = lax.axis_index("dp")
        y_arr = (d // NC).astype(jnp.int32)[None]
        c_arr = (d % NC).astype(jnp.int32)[None]

        own = pack(tokens, cotangent, routes, route_gain)
        a, c_mid = hop1(own)

        own_ids = z * nx + (x ^ jnp.arange(nx, dtype=jnp.int32))
        alive = jnp.sum(
            jnp.where(
                own_ids[:, None] == jnp.arange(experts_all)[None, :], expert_alive[None, :], 0
            ),
            axis=1,
        )
        ids = jnp.stack([own_ids, alive.astype(jnp.int32)])

        def pick(metas, xs=(), cs=()):
            own, sends = pick_rows(ids, metas, xs, cs, nx, cap, top, width, tok_count)
            return own, over_x(sends)

        xs, ds, hidden, cot_rows = [], [], [], []

        def spread(pieces, values):
            got = [over_y(values[k], k) for k in range(1, ny)]
            pieces += [values[0], *got]
            return got

        def forward(parts):
            gate, up, *splits = gate_up(y_arr, parts, w_gate, w_up, ny)
            return gate, up, spread(xs, splits)

        def backward(parts, gate, up):
            both, hid, cot = back(parts, w_down, gate, up)
            hidden.append(hid)
            cot_rows.append(cot)
            return both, spread(ds, [both] * ny)

        x0, s0 = pick([own], [own])
        c0, t0 = pick([own], (), [after(own, x0)])
        g0, u0, xs0 = forward([x0, *s0])
        f0, d0 = backward([c0, *t0], g0, u0)
        a, c_mid = after((a, c_mid), f0)
        b_end, b_mid = hop2(a, c_mid)
        x1, s1 = pick([a], [a])
        c1, t1 = pick([a], (), [after(a, x1)])
        s1 = after(s1, c1, xs0)
        g1, u1, xs1 = forward([x1, *s1])
        t1 = after(t1, d0)
        f1, d1 = backward([c1, *t1], g1, u1)
        xc_end = hop3(b_mid[:tok_count])
        cc_end = hop3(b_mid[tok_count:, :width])
        b_end, b_mid = after((b_end, b_mid), f1)
        x2, s2 = pick([b_end, b_mid], [b_end, b_mid])
        c2, t2 = pick([b_end, b_mid], (), after([b_end, b_mid], x2))
        s2 = after(s2, c2, xs1)
        g2, u2, xs2 = forward([x2, *s2])
        c_mid, xc_end = after((c_mid, xc_end), g2)
        x3, s3 = pick([c_mid, xc_end], [c_mid, xc_end])
        t2 = after(t2, x3, d1)
        f2, d2 = backward([c2, *t2], g2, u2)
        cc_end = after(cc_end, f2)
        c3, t3 = pick([c_mid, xc_end], (), [c_mid, cc_end])
        s3 = after(s3, c3)
        g3, u3, xs3 = forward([x3, *s3])
        t3 = after(t3, xs2, d2)
        f3, d3 = backward([c3, *t3], g3, u3)

        n = ff // n_dp
        hidden = after(hidden, xs3)

        def to_core(yy):
            return over_core(down_part(yy * NC + (1 - c_arr), hidden, cot_rows, n)[0])

        if ny == 2:
            other = jnp.concatenate([(y_arr ^ k) * NC + (1 - c_arr) for k in (1, 0)])
            first, second = down_sends(other, hidden, cot_rows, n)
            sent, own_recv = [over_core(first)], over_core(second)
        else:
            sent = [to_core(y_arr ^ k) for k in range(1, ny)]
            own_recv = to_core(y_arr)
        landed, totals = [], []
        for k in range(1, ny):
            recv = sent[k - 1]
            (total,) = down_part((y_arr ^ k) * NC + c_arr, hidden, cot_rows, n, [[after(recv, own_recv)]])
            landed.append([over_y(total, k)])
            totals.append(total)

        m = half // NC
        if m % LANES == 0:
            ds[0] = after(ds[0], totals)
            recv = [over_core(v) for v in both_part(1 - c_arr, xs, ds, m)]
            grad_gate, grad_up = both_part(c_arr, xs, ds, m, recv)
        else:
            x_all = jnp.concatenate(xs, axis=0)
            d_all = jnp.concatenate(ds, axis=0)

            def part(c):
                return contract_rows(lax.dynamic_slice_in_dim(x_all, c * m, m, 1), d_all)

            recv = over_core(part(1 - c_arr[0]).astype(BF16))
            total = (part(c_arr[0]) + recv.astype(F32)).astype(BF16)
            grad_gate, grad_up = total[:, :ff], total[:, ff:]

        (kept,) = down_part(
            y_arr * NC + c_arr, hidden, cot_rows, n, [[own_recv]], dtype=F32
        )
        landed = after(landed, kept, grad_up)
        for (part,) in landed:
            kept = kept + part.astype(F32)
        grad_down = kept.astype(BF16)
        return grad_gate[None], grad_up[None], grad_down[None]

    return per_device


def solution(mesh):
    in_specs = (
        P(("dp", "expert"), None),
        P(("dp", "expert"), None),
        P(("dp", "expert"), None),
        P(("dp", "expert"), None),
        P(),
        P("expert", None, None),
        P("expert", None, None),
        P("expert", None, None),
    )
    out_specs = (P("expert", "dp", None), P("expert", "dp", None), P("expert", "dp", None))
    per_device = make_per_device(mesh.shape["dp"], mesh.shape["expert"])
    return jax.shard_map(
        per_device, mesh=mesh, in_specs=in_specs, out_specs=out_specs, check_vma=False
    )
```
